32 devices in a mesh: groups: 2 (over y), streams: 8 (over z, x), segment: 2 (over core).
Axes of the slice: x: 2, y: 2, z: 4, core: 2. Of those that a mesh axis runs over, the one named last changes fastest.
Arguments:
- latent: bfloat16 [4096, 1024], P(('groups', 'streams'), 'segment'), parts along dimension 0, may hold values from -6 to 6
- conv_weight: bfloat16 [1024, 16, 512], P('streams', None, 'segment'), may hold values from -0.1875 to 0.1875
- conv_bias: float32 [512], P('segment'), may hold values from -3 to 3
- tail_cache: bfloat16 [128, 8, 512], P(('groups', 'streams'), None, 'segment'), parts along dimension 0, may hold values from -6 to 6
- input_cache: bfloat16 [128, 2, 512], P(('groups', 'streams'), None, 'segment'), parts along dimension 0, may hold values from -0.8984375 to 2
- resume_slot: int32 [128], P(('groups', 'streams')), parts along dimension 0, may hold values from -1 to 255, as said below
- res_weight: bfloat16 [3, 512, 256], P(None, 'segment'), may hold values from -0.15625 to 0.15625
- res_bias: float32 [256], replicated, may hold values from -3 to 3
- skip_weight: bfloat16 [256, 512], P(None, 'segment'), may hold values from -0.375 to 0.375
- skip_bias: float32 [512], P('segment'), may hold values from -3 to 3
Outputs:
- decoded: bfloat16 [4096, 8, 512], P(('groups', 'streams'), None, 'segment'), parts along dimension 0
- new_tail: bfloat16 [4096, 8, 512], P(('groups', 'streams'), None, 'segment'), parts along dimension 0
The draws below stay inside these ranges and needn't reach their ends.
There are 2 independent parts, one for each index of `groups`. The reference program is written for one: setup_inputs(seed, part) draws one part's arguments, and reference() takes and returns one part's arrays. A program takes and returns all parts, laid end to end along the dimension named above; an argument that names none is the same for every part. Nothing has to cross between parts.
Inputs may be any that keep to these rules, and one draw needn't show every extreme that they name: `resume_slot`: slot k of an owner device's store serves decoder device k // 1 of the same index range; an entry is -1 (slot unused) or the position, among that decoder device's 256 rows in decoder order, of the session that resumes from it. No decoder row is named by two slots. In every draw there is one decoder device all of whose reserved slots are in use (none is -1).
All inputs are finite; a program needn't handle non-finite values.
Results may differ from the reference program's by a relative error of at most 0.0042.
Values may be sent and summed in bfloat16 or wider, within the bound.
A program may use at most 64 MiB of HBM per device.

```python
import jax
import jax.numpy as jnp
from jax import lax

D = 1024
C1 = 512
HID = 256
STRIDE = 8
RES_K = 3
CAP = 1
S_DEV = 256
KERNEL = 16
SESSIONS = 2048
SLOTS = 64
N_STREAMS = 8


def draw_resume_slot(key, part):
    incoming_count = N_STREAMS * CAP
    device_keys = jax.random.split(jax.random.fold_in(key, 11), N_STREAMS)
    orders = jax.vmap(lambda single: jax.random.permutation(single, S_DEV))(device_keys)
    incoming = orders[:, :incoming_count].astype(jnp.int32)
    full_device = jax.random.randint(jax.random.fold_in(key, 12), (), 0, N_STREAMS)
    device_ids = jnp.arange(N_STREAMS, dtype=jnp.int32)[:, None]
    offsets = jnp.where(device_ids == full_device, S_DEV - 1 - incoming[:, :1], 0)
    incoming = (incoming + offsets) % S_DEV
    coins = jax.random.randint(jax.random.fold_in(key, 13), (N_STREAMS, incoming_count), 0, 2)
    used = (coins == 1) | (device_ids == full_device)
    named = jnp.where(used, incoming, -1)
    named = named.reshape(N_STREAMS, N_STREAMS, CAP).transpose(1, 0, 2)
    return named.reshape(-1).astype(jnp.int32)


def levels(rng, dims, cuts, low, top_value):
    loudness, own = 1.0, jax.random.fold_in(rng, 6)
    for position, blocks in cuts:
        heights = jnp.exp(jax.random.uniform(jax.random.fold_in(own, position), (blocks,), jnp.float32, low / len(cuts), top_value / len(cuts)))
        loudness = loudness * jnp.repeat(heights, dims[position] // blocks).reshape([-1 if axis == position else 1 for axis in range(len(dims))])
    return loudness


def noise(key, shape, scale, bound, cuts=(), held_as=jnp.bfloat16):
    drawn = scale * jax.random.normal(key, shape, jnp.float32)
    if cuts:
        drawn = drawn * levels(key, shape, cuts, -0.22, 0.18)
    return jnp.clip(drawn, -bound, bound).astype(held_as)


def setup_inputs(seed: int = 0, part: int = 0) -> dict:
    streams_of = jax.random.split(jax.random.key(seed), 11)
    part_splits = jax.random.split(jax.random.fold_in(streams_of[10], part), 11)
    latent = noise(part_splits[0], (SESSIONS, D), 1.0, 6.0, ((0, 8), (1, 2)))
    conv_weight = noise(streams_of[1], (D, KERNEL, C1), D ** -0.5, 0.1875, ((0, 8), (2, 2)))
    conv_bias = noise(streams_of[2], (C1,), 0.5, 3.0, ((0, 2),), jnp.float32)
    tail_cache = noise(part_splits[3], (SLOTS, STRIDE, C1), 1.0, 6.0, ((0, 8), (2, 2)))
    input_cache = jnp.clip(-0.8984375 + 2.8984375 * jax.random.uniform(part_splits[4], (SLOTS, RES_K - 1, C1), jnp.float32) ** levels(part_splits[4], (SLOTS, RES_K - 1, C1), ((0, 8), (2, 2)), -0.2, 0.2), -0.8984375, 2.0).astype(jnp.bfloat16)
    resume_slot = draw_resume_slot(jax.random.fold_in(jax.random.fold_in(streams_of[10], part), 71), part)
    res_weight = noise(streams_of[6], (RES_K, C1, HID), (RES_K * C1) ** -0.5, 0.15625, ((1, 2),))
    res_bias = noise(streams_of[7], (HID,), 0.5, 3.0, (), jnp.float32)
    skip_weight = noise(streams_of[8], (HID, C1), HID ** -0.5, 0.375, ((1, 2),))
    skip_bias = noise(streams_of[9], (C1,), 0.5, 3.0, ((0, 2),), jnp.float32)
    return dict(latent=latent, conv_weight=conv_weight, conv_bias=conv_bias, tail_cache=tail_cache, input_cache=input_cache, resume_slot=resume_slot, res_weight=res_weight, res_bias=res_bias, skip_weight=skip_weight, skip_bias=skip_bias)


def apply_elu(values):
    return jnp.where(values > 0, values, jnp.expm1(jnp.minimum(values, 0.0)))


def reference(latent, conv_weight, conv_bias, tail_cache, input_cache, resume_slot, res_weight, res_bias, skip_weight, skip_bias):
    lanes = N_STREAMS
    portion = S_DEV // lanes
    ordered = latent.reshape(lanes, lanes, portion, D).transpose(1, 0, 2, 3).reshape(lanes, S_DEV, D)
    tails = tail_cache.reshape(lanes, lanes, CAP, STRIDE * C1).transpose(1, 0, 2, 3).reshape(lanes, lanes * CAP, STRIDE * C1)
    inputs = input_cache.reshape(lanes, lanes, CAP, (RES_K - 1) * C1).transpose(1, 0, 2, 3).reshape(lanes, lanes * CAP, (RES_K - 1) * C1)
    slots = resume_slot.reshape(lanes, lanes, CAP).transpose(1, 0, 2).reshape(lanes, lanes * CAP)
    kernel_flat = conv_weight.reshape(D, KERNEL * C1)
    positions = jnp.arange(S_DEV, dtype=jnp.int32)

    def one_block(block):
        rows_in, tail_rows, input_rows, slot_rows = block
        excitation = apply_elu(rows_in.astype(jnp.float32)).astype(jnp.bfloat16)
        spread = jnp.dot(excitation, kernel_flat, preferred_element_type=jnp.float32).reshape(S_DEV, KERNEL, C1)
        one_hot = (slot_rows[None, :] == positions[:, None]).astype(jnp.bfloat16)
        prev_tail = jnp.dot(one_hot, tail_rows, preferred_element_type=jnp.float32).reshape(S_DEV, STRIDE, C1)
        prev_input = jnp.dot(one_hot, input_rows, preferred_element_type=jnp.float32).reshape(S_DEV, RES_K - 1, C1)
        upsampled = spread[:, :STRIDE] + prev_tail + conv_bias
        carried = spread[:, STRIDE:].astype(jnp.bfloat16)
        excited = apply_elu(upsampled).astype(jnp.bfloat16)
        window = jnp.concatenate([prev_input.astype(jnp.bfloat16), excited], axis=1).astype(jnp.float32)
        branch = jnp.zeros((S_DEV, STRIDE, HID), jnp.float32) + res_bias
        for offset in range(RES_K):
            branch = branch + jnp.einsum("stc,ch->sth", window[:, offset:offset + STRIDE], res_weight[offset].astype(jnp.float32))
        hidden = apply_elu(branch).astype(jnp.bfloat16)
        mixed = upsampled + jnp.einsum("sth,hc->stc", hidden.astype(jnp.float32), skip_weight.astype(jnp.float32)) + skip_bias
        return mixed.astype(jnp.bfloat16), carried

    decoded, new_tail = lax.map(one_block, (ordered, tails, inputs, slots))
    return decoded.reshape(lanes * S_DEV, STRIDE, C1), new_tail.reshape(lanes * S_DEV, STRIDE, C1)
```

```python
import jax
import jax.numpy as jnp
from jax import lax
from jax.experimental import pallas as pl
from jax.experimental.pallas import tpu as pltpu
from jax.sharding import PartitionSpec as P


def apply_elu(values):
    return jnp.where(values > 0, values, jnp.expm1(jnp.minimum(values, 0.0)))


def local(
    latent,
    conv_weight,
    conv_bias,
    tail_cache,
    input_cache,
    resume_slot,
    res_weight,
    res_bias,
    skip_weight,
    skip_bias,
):
    handed = lax.all_to_all(latent, "streams", split_axis=0, concat_axis=0, tiled=True)
    excitation_half = apply_elu(handed.astype(jnp.float32)).astype(jnp.bfloat16)
    excitation = lax.all_gather(excitation_half, "segment", axis=1, tiled=True)
    session_rows = excitation.shape[0]
    tap_count = conv_weight.shape[1]
    half_taps = tap_count // 2
    half_width = conv_weight.shape[2]
    piece = lax.all_gather(conv_weight, "streams", axis=0, tiled=True)
    kernel_rows = piece.reshape(piece.shape[0], tap_count * half_width)
    spread = jnp.dot(excitation, kernel_rows, preferred_element_type=jnp.float32)
    spread = spread.reshape(session_rows, tap_count, half_width)
    fetched_tail, fetched_input, fetched_slot = (
        lax.all_to_all(tail_cache, "streams", split_axis=0, concat_axis=0, tiled=True),
        lax.all_to_all(input_cache, "streams", split_axis=0, concat_axis=0, tiled=True),
        lax.all_to_all(resume_slot, "streams", split_axis=0, concat_axis=0, tiled=True),
    )
    arrivals = fetched_slot.shape[0]
    state_steps = fetched_input.shape[1]
    packed = jnp.concatenate(
        [fetched_tail.reshape(arrivals, -1), fetched_input.reshape(arrivals, -1)], axis=1
    )
    one_hot = (fetched_slot[None, :] == jnp.arange(session_rows, dtype=jnp.int32)[:, None]).astype(
        jnp.bfloat16
    )
    placed = jnp.dot(one_hot, packed, preferred_element_type=jnp.float32)
    prev_tail = placed[:, : half_taps * half_width].reshape(session_rows, half_taps, half_width)
    prev_input = (
        placed[:, half_taps * half_width :]
        .reshape(session_rows, state_steps, half_width)
        .astype(jnp.bfloat16)
    )
    upsampled = spread[:, :half_taps] + prev_tail + conv_bias
    new_tail = spread[:, half_taps:].astype(jnp.bfloat16)
    excited = apply_elu(upsampled).astype(jnp.bfloat16)
    window = jnp.concatenate([prev_input, excited], axis=1)
    hidden_width = res_weight.shape[2]
    partial_value = jnp.zeros((session_rows * half_taps, hidden_width), jnp.float32)
    for offset in range(res_weight.shape[0]):
        frames = window[:, offset : offset + half_taps].reshape(
            session_rows * half_taps, half_width
        )
        partial_value = partial_value + jnp.dot(
            frames, res_weight[offset], preferred_element_type=jnp.float32
        )
    partial_value = partial_value.reshape(session_rows, half_taps, hidden_width)
    summed = lax.psum(partial_value, "segment")
    hidden = apply_elu(summed + res_bias).astype(jnp.bfloat16)
    projected = jnp.dot(
        hidden.reshape(session_rows * half_taps, hidden_width),
        skip_weight,
        preferred_element_type=jnp.float32,
    )
    decoded_block = upsampled + projected.reshape(session_rows, half_taps, half_width) + skip_bias
    return (decoded_block.astype(jnp.bfloat16), new_tail)


UNITS = 8
AHEAD = 3
MESH = pl.DeviceIdType.MESH


def elu32(values):
    return jnp.where(values > 0, values, jnp.exp(jnp.minimum(values, 0.0)) - 1.0)


def fused_kernel(
    lat_ref, w_ref, tailc_ref, inpc_ref, slot_hbm, convb_hbm, resw_ref, resb_hbm, skipw_ref, skipb_hbm,
    dec_ref, tail_ref,
    wbuf, lst, exc, pack, cach, spin, outbox, ups, win, resbuf, match, slots, convb, resb, skipb,
    w_send, w_recv, x_send, x_recv, l_send, l_recv, sx_send, sx_recv, sy_send, sy_recv,
    half_send, half_recv, c_send, c_recv, win_send, win_recv, out_send, out_recv, sl_sem, local_sem,
):
    g = lax.axis_index("groups")
    j = lax.axis_index("streams")
    c = lax.axis_index("segment")
    z, x = j // 2, lax.rem(j, 2)
    jx = z * 2 + 1 - x
    mine = 2 * g + x
    theirs = 2 * g + 1 - x
    f32, bf16 = jnp.float32, jnp.bfloat16

    def at(gg, jj, cc):
        return {"groups": gg, "streams": jj, "segment": cc}

    def remote(src, dst, ss, rs, dev):
        return pltpu.make_async_remote_copy(
            src_ref=src, dst_ref=dst, send_sem=ss, recv_sem=rs, device_id=dev, device_id_type=MESH
        )

    partner = at(g, j, 1 - c)
    side = at(g, jx, c)
    across = at(1 - g, j, c)
    corner = at(1 - g, jx, c)
    above = at(g, j + 2, c)
    below = at(g, j - 2, c)
    has_up, has_down = z < 3, z > 0

    barrier = pltpu.get_barrier_semaphore()

    def greet(dev):
        pl.semaphore_signal(barrier, inc=1, device_id=dev, device_id_type=MESH)

    greet(side)
    greet(across)
    greet(partner)
    pl.when(has_up)(lambda: greet(above))
    pl.when(has_down)(lambda: greet(below))

    own_w = pltpu.make_async_copy(
        w_ref.at[mine], wbuf.at[:, pl.ds(j * 128, 128)], local_sem.at[0]
    )
    own_res = pltpu.make_async_copy(resw_ref, resbuf.at[c], local_sem.at[1])
    small = [
        pltpu.make_async_copy(slot_hbm, slots, local_sem.at[2]),
        pltpu.make_async_copy(convb_hbm, convb, local_sem.at[3]),
        pltpu.make_async_copy(resb_hbm, resb, local_sem.at[4]),
        pltpu.make_async_copy(skipb_hbm, skipb, local_sem.at[5]),
    ]
    own_w.start()
    own_res.start()
    for copy in small:
        copy.start()
    lst[z] = elu32(lat_ref[...].astype(f32)).astype(bf16).reshape(4, 2, 32, 512)

    pl.semaphore_wait(barrier, 3 + jnp.where(has_up, 1, 0) + jnp.where(has_down, 1, 0))

    def l_copy(s, d, up):
        block = lst.at[z - s if up else z + s, d]
        k = 0 if up else 1
        return remote(block, block, l_send.at[k, s, d], l_recv.at[k, s, d], above if up else below)

    def l_arrival(s, d, up):
        block = lst.at[z - 1 - s if up else z + 1 + s, d]
        k = 0 if up else 1
        return remote(block, block, l_send.at[k, s, d], l_recv.at[k, s, d], below if up else above)

    def share_side(o):
        return remote(lst.at[o, z], exc.at[g, c, :, o, x], sx_send.at[o], sx_recv.at[o], side)

    def share_across(o):
        return remote(lst.at[o, z], exc.at[g, c, :, o, x], sy_send.at[o], sy_recv.at[o], across)

    def share_here(o):
        return pltpu.make_async_copy(lst.at[o, z], exc.at[g, c, :, o, x], sl_sem.at[o])

    def share(o):
        share_side(o).start()
        share_across(o).start()
        share_here(o).start()

    def relay_copy(o):
        block = exc.at[g, c, :, o, 1 - x]
        return remote(block, block, sy_send.at[4 + o], sy_recv.at[4 + o], across)

    def relay(o):
        block = exc.at[g, c, :, o, 1 - x]
        remote(block, block, sx_send.at[o], sx_recv.at[o], side).wait_recv()
        relay_copy(o).start()

    def l_step(s):
        @pl.when(z - 1 - s >= 0)
        def _():
            for d in range(3, s, -1):

                @pl.when(d >= z)
                def _():
                    l_arrival(s, d, True).wait_recv()

                if d >= s + 2:

                    @pl.when(d > z)
                    def _():
                        l_copy(s + 1, d, True).start()

            share(z - 1 - s)

        @pl.when(z + 1 + s <= 3)
        def _():
            for d in range(0, 3 - s):

                @pl.when(d <= z)
                def _():
                    l_arrival(s, d, False).wait_recv()

                if d <= 1 - s:

                    @pl.when(d < z)
                    def _():
                        l_copy(s + 1, d, False).start()

            share(z + 1 + s)

    def relay_step(s):
        pl.when(z - 1 - s >= 0)(lambda: relay(z - 1 - s))
        pl.when(z + 1 + s <= 3)(lambda: relay(z + 1 + s))

    def cross(n):
        return remote(
            w_ref.at[theirs, n], wbuf.at[n, pl.ds(j * 128, 128)], x_send.at[n], x_recv.at[n], side
        )

    def plain(n, up):
        k = 0 if up else 1
        return remote(
            w_ref.at[mine, n], wbuf.at[n, pl.ds(j * 128, 128)], w_send.at[n, k, 0], w_recv.at[n, k, 0],
            above if up else below,
        )

    def crossed(n, up):
        k = 0 if up else 1
        block = wbuf.at[n, pl.ds(jx * 128, 128)]
        return remote(block, block, w_send.at[n, k, 1], w_recv.at[n, k, 0], above if up else below)

    def passed(n, s, up):
        k = 0 if up else 1
        block = wbuf.at[n, pl.ds((z - s if up else z + s) * 256, 256)]
        return remote(block, block, w_send.at[n, k, 1 + s], w_recv.at[n, k, s], above if up else below)

    def arrival(n, s, up):
        k = 0 if up else 1
        block = wbuf.at[n, pl.ds((z - 1 - s if up else z + 1 + s) * 256, 256)]
        return remote(block, block, w_send.at[n, k, 1 + s], w_recv.at[n, k, s], below if up else above)

    def send_plain(n):
        pl.when(has_up)(lambda: plain(n, True).start())
        pl.when(has_down)(lambda: plain(n, False).start())

    def send_crossed(n):
        block = wbuf.at[n, pl.ds(jx * 128, 128)]
        remote(block, block, x_send.at[n], x_recv.at[n], side).wait_recv()
        pl.when(has_up)(lambda: crossed(n, True).start())
        pl.when(has_down)(lambda: crossed(n, False).start())

    def forward(n, s):
        @pl.when(z - 1 - s >= 0)
        def _():
            arrival(n, s, True).wait_recv()
            if s < 2:
                pl.when(has_up)(lambda: passed(n, s + 1, True).start())

        @pl.when(z + 1 + s <= 3)
        def _():
            arrival(n, s, False).wait_recv()
            if s < 2:
                pl.when(has_down)(lambda: passed(n, s + 1, False).start())

    def pump(tick):
        for s in (2, 1, 0):
            if 0 <= tick - s < UNITS:
                forward(tick - s, s)
        n = tick + AHEAD
        if n < UNITS:
            send_plain(n)
            send_crossed(n)
        if n + 2 < UNITS:
            cross(n + 2).start()

    for d in (3, 2, 1):
        pl.when(d > z)(lambda d=d: l_copy(0, d, True).start())
    for d in (0, 1, 2):
        pl.when(d < z)(lambda d=d: l_copy(0, d, False).start())
    cross(0).start()
    cross(1).start()
    share(z)
    send_plain(0)
    send_plain(1)
    for n in range(2, AHEAD + 2):
        cross(n).start()
    res_out = remote(resw_ref, resbuf.at[c], half_send.at[2], half_recv.at[2], partner)
    res_in = remote(resw_ref, resbuf.at[1 - c], half_send.at[2], half_recv.at[2], partner)
    res_out.start()

    for copy in small:
        copy.wait()
    for d in range(8):
        pack[d] = jnp.concatenate(
            [
                tailc_ref[d].astype(f32),
                inpc_ref[d].astype(f32),
                jnp.full((6, 256), slots[d].astype(f32)),
            ],
            axis=0,
        ).astype(bf16)

    send_crossed(0)
    send_crossed(1)
    l_step(0)
    relay(z)
    for n in range(2, AHEAD):
        send_plain(n)
        send_crossed(n)
    pump(0)
    l_step(1)
    relay_step(0)
    pump(1)
    l_step(2)
    relay_step(1)
    pump(2)
    relay_step(2)

    def half_copy(gg, index):
        return remote(
            exc.at[gg, c], exc.at[gg, c], half_send.at[index], half_recv.at[index], partner
        )

    def half_arrival(gg, index):
        return remote(
            exc.at[gg, 1 - c], exc.at[gg, 1 - c], half_send.at[index], half_recv.at[index], partner
        )

    for o in range(4):
        share_here(o).wait()
    half_copy(g, 0).start()

    def cache_copy(d):
        peer = lax.rem(j + d, 8)
        return remote(pack.at[peer], cach.at[j], c_send.at[d], c_recv.at[d], at(g, peer, c))

    def cache_arrival(d):
        peer = lax.rem(j + 8 - d, 8)
        return remote(pack.at[0], cach.at[peer], c_send.at[d], c_recv.at[d], at(g, peer, c))

    for d in range(1, 8):
        cache_copy(d).start()
    cach[j] = pack[j]

    for o in range(4):
        for k, xx in ((0, x), (4, 1 - x)):
            block = exc.at[1 - g, c, :, o, xx]
            remote(block, block, sy_send.at[k + o], sy_recv.at[k + o], across).wait_recv()
    half_copy(1 - g, 1).start()
    pump(3)
    own_w.wait()
    half_arrival(g, 0).wait_recv()
    half_arrival(1 - g, 1).wait_recv()

    routes = {1: (g, 1 - x, side), 2: (1 - g, x, across), 3: (1 - g, 1 - x, corner)}

    def out_block(i, lanes, quarter):
        if i < 2:
            return spin.at[4 * i + quarter]
        if i == 2:
            return tail_ref.at[quarter]
        return tail_ref.at[4 + quarter, :, lanes]

    def out_copy(r, k):
        i, lanes = parts[k]
        gg, xx, dev = routes[r]
        src = outbox.at[r - 1, i] if i < 3 else outbox.at[r - 1, i, :, lanes]
        return remote(src, out_block(i, lanes, mine), out_send.at[r, k], out_recv.at[r, k], dev)

    def out_arrival(r, k):
        i, lanes = parts[k]
        gg, xx, dev = routes[r]
        block = out_block(i, lanes, 2 * gg + xx)
        return remote(block, block, out_send.at[r, k], out_recv.at[r, k], dev)

    whole = slice(0, 256)
    parts = [(0, whole), (1, whole), (2, whole), (3, slice(0, 128)), (3, slice(128, 256))]

    def spread_of(gg, xx, k):
        i, lanes = parts[k]
        if i < 3:
            low = jnp.concatenate([wbuf[2 * i, :512], wbuf[2 * i + 1, :512]], axis=1)
            high = jnp.concatenate([wbuf[2 * i, 512:], wbuf[2 * i + 1, 512:]], axis=1)
        else:
            low, high = wbuf[3 + k, :512], wbuf[3 + k, 512:]
        value = jnp.dot(exc[gg, 0, xx].reshape(256, 512), low, preferred_element_type=f32)
        value += jnp.dot(exc[gg, 1, xx].reshape(256, 512), high, preferred_element_type=f32)
        return value.astype(bf16)

    def produce(k):
        i, lanes = parts[k]
        for r in (3, 1, 2):
            gg, xx, dev = routes[r]
            outbox[r - 1, i, :, lanes] = spread_of(gg, xx, k)
            out_copy(r, k).start()
        value = spread_of(g, x, k)
        if i < 2:
            spin[4 * i + mine] = value
        elif i == 2:
            tail_ref[mine] = value
        else:
            tail_ref[4 + mine, :, lanes] = value

    def placed(row):
        lanes = lax.broadcasted_iota(jnp.int32, (256, 128), 1)
        chosen = jnp.where(lax.rem(lanes, 16) == row, match[...], 0.0).astype(bf16)
        return jnp.dot(chosen, cach[...].reshape(128, 256), preferred_element_type=f32)

    def win_rows(i):
        return pl.ds(0, 6) if i == 0 else pl.ds(6, 4)

    def win_copy(i):
        block = win.at[c, win_rows(i)]
        return remote(block, block, win_send.at[i], win_recv.at[i], partner)

    def win_arrival(i):
        block = win.at[1 - c, win_rows(i)]
        return remote(block, block, win_send.at[i], win_recv.at[i], partner)

    def upsample(i):
        for r in (1, 2, 3):
            out_arrival(r, i).wait_recv()

        @pl.loop(4 * i, 4 * i + 4)
        def _(t):
            value = spin[t].astype(f32) + placed(t) + convb[...]
            ups[t] = value
            win[c, t + 2] = elu32(value).astype(bf16)

        win_copy(i).start()

    def decode(i):
        win_arrival(i).wait_recv()

        @pl.loop(0, 2)
        def _(p):
            t = 4 * i + 2 * p
            branch = jnp.zeros((512, 256), f32) + resb[...]
            for k in range(3):
                for h in range(2):
                    branch = branch + jnp.dot(
                        win[h, pl.ds(t + k, 2)].reshape(512, 256), resbuf[h, k],
                        preferred_element_type=f32,
                    )
            hidden = elu32(branch).astype(bf16)
            value = ups[pl.ds(t, 2)].reshape(512, 256) + jnp.dot(
                hidden, skipw_ref[...], preferred_element_type=f32
            ) + skipb[...]
            dec_ref[pl.ds(t, 2)] = value.astype(bf16).reshape(2, 256, 256)

    produce(0)
    pump(4)
    own_res.wait()
    res_in.wait_recv()
    for d in range(1, 8):
        cache_arrival(d).wait_recv()
    named = jnp.broadcast_to(cach[...].astype(f32)[:, 10:11, :], (8, 16, 256)).reshape(128, 256)
    sessions = lax.broadcasted_iota(jnp.int32, (128, 256), 1).astype(f32)
    match[...] = jnp.where(named == sessions, 1.0, 0.0).T
    for i in range(2):
        win[c, i] = placed(8 + i).astype(bf16)
    pump(5)
    produce(1)
    upsample(0)
    pump(6)
    decode(0)
    pump(7)
    produce(2)
    upsample(1)
    pump(8)
    produce(3)
    decode(1)
    pump(9)
    produce(4)

    for k in range(2, 5):
        for r in (1, 2, 3):
            out_arrival(r, k).wait_recv()

    for k in range(5):
        for r in (1, 2, 3):
            out_copy(r, k).wait_send()
    for i in range(2):
        win_copy(i).wait_send()
        half_copy((g, 1 - g)[i], i).wait_send()
    res_out.wait_send()
    for d in range(1, 8):
        cache_copy(d).wait_send()
    for o in range(4):
        share_side(o).wait_send()
        share_across(o).wait_send()
        relay_copy(o).wait_send()
    for s in range(3):
        for d in range(4):
            if d >= s + 1:
                pl.when((z - s >= 0) & (d > z))(lambda s=s, d=d: l_copy(s, d, True).wait_send())
            if d <= 2 - s:
                pl.when((z + s <= 3) & (d < z))(lambda s=s, d=d: l_copy(s, d, False).wait_send())

    @pl.loop(0, UNITS)
    def _(n):
        cross(n).wait_send()
        for up, has in ((True, has_up), (False, has_down)):

            @pl.when(has)
            def _():
                plain(n, up).wait_send()
                crossed(n, up).wait_send()
                for s in (1, 2):
                    pl.when((z - s >= 0) if up else (z + s <= 3))(
                        lambda s=s: passed(n, s, up).wait_send()
                    )


def fused(
    latent, conv_weight, conv_bias, tail_cache, input_cache, resume_slot,
    res_weight, res_bias, skip_weight, skip_bias,
):
    quarters = conv_weight.reshape(128, 4, 4, 2, 128).transpose(2, 1, 3, 0, 4).reshape(4, 8, 128, 128)
    dma = pltpu.SemaphoreType.DMA
    bf16, f32 = jnp.bfloat16, jnp.float32
    vmem = pl.BlockSpec(memory_space=pltpu.VMEM)
    anywhere = pl.BlockSpec(memory_space=pl.ANY)
    decoded, new_tail = pl.pallas_call(
        fused_kernel,
        out_shape=(
            jax.ShapeDtypeStruct((8, 256, 256), bf16),
            jax.ShapeDtypeStruct((8, 256, 256), bf16),
        ),
        in_specs=[
            vmem, vmem, vmem, vmem, anywhere, anywhere, vmem, anywhere, vmem, anywhere,
        ],
        out_specs=(vmem,) * 2,
        scratch_shapes=[
            pltpu.VMEM((8, 1024, 128), bf16),
            pltpu.VMEM((4, 4, 2, 32, 512), bf16),
            pltpu.VMEM((2, 2, 2, 4, 2, 32, 512), bf16),
            pltpu.VMEM((8, 16, 256), bf16),
            pltpu.VMEM((8, 16, 256), bf16),
            pltpu.VMEM((8, 256, 256), bf16),
            pltpu.VMEM((3, 4, 256, 256), bf16),
            pltpu.VMEM((8, 256, 256), f32),
            pltpu.VMEM((2, 10, 256, 256), bf16),
            pltpu.VMEM((2, 3, 256, 256), bf16),
            pltpu.VMEM((256, 128), f32),
            pltpu.SMEM((8,), jnp.int32),
            pltpu.VMEM((1, 256), f32),
            pltpu.VMEM((1, 256), f32),
            pltpu.VMEM((1, 256), f32),
            dma((8, 2, 4)), dma((8, 2, 3)),
            dma((8,)), dma((8,)),
            dma((2, 3, 4)), dma((2, 3, 4)),
            dma((4,)), dma((4,)),
            dma((8,)), dma((8,)),
            dma((3,)), dma((3,)),
            dma((8,)), dma((8,)),
            dma((2,)), dma((2,)),
            dma((4, 5)), dma((4, 5)),
            dma((4,)), dma((6,)),
        ],
        compiler_params=pltpu.CompilerParams(
            collective_id=0, has_side_effects=True, vmem_limit_bytes=48 * 1024 * 1024
        ),
    )(
        latent, quarters, tail_cache, input_cache, resume_slot, conv_bias[None, :], res_weight,
        res_bias[None, :], skip_weight, skip_bias[None, :],
    )
    return decoded.transpose(1, 0, 2), new_tail.transpose(1, 0, 2)


def solution(mesh):
    sizes = tuple(mesh.shape[name] for name in ("groups", "streams", "segment"))
    body = fused if sizes == (2, 8, 2) else local
    placed = (
        P(("groups", "streams"), "segment"),
        P("streams", None, "segment"),
        P("segment"),
        P(("groups", "streams"), None, "segment"),
        P(("groups", "streams"), None, "segment"),
        P(("groups", "streams")),
        P(None, "segment", None),
        P(),
        P(None, "segment"),
        P("segment"),
    )
    return jax.shard_map(
        body,
        mesh=mesh,
        in_specs=placed,
        out_specs=(
            P(("groups", "streams"), None, "segment"),
            P(("groups", "streams"), None, "segment"),
        ),
        check_vma=False,
    )
```

```python
import jax
import jax.numpy as jnp
from jax import lax
from jax.experimental import pallas as pl
from jax.experimental.pallas import tpu as pltpu
from jax.sharding import PartitionSpec as P


def apply_elu(values):
    return jnp.where(values > 0, values, jnp.expm1(jnp.minimum(values, 0.0)))


def local(
    latent,
    conv_weight,
    conv_bias,
    tail_cache,
    input_cache,
    resume_slot,
    res_weight,
    res_bias,
    skip_weight,
    skip_bias,
):
    handed = lax.all_to_all(latent, "streams", split_axis=0, concat_axis=0, tiled=True)
    excitation_half = apply_elu(handed.astype(jnp.float32)).astype(jnp.bfloat16)
    excitation = lax.all_gather(excitation_half, "segment", axis=1, tiled=True)
    session_rows = excitation.shape[0]
    tap_count = conv_weight.shape[1]
    half_taps = tap_count // 2
    half_width = conv_weight.shape[2]
    piece = lax.all_gather(conv_weight, "streams", axis=0, tiled=True)
    kernel_rows = piece.reshape(piece.shape[0], tap_count * half_width)
    spread = jnp.dot(excitation, kernel_rows, preferred_element_type=jnp.float32)
    spread = spread.reshape(session_rows, tap_count, half_width)
    fetched_tail, fetched_input, fetched_slot = (
        lax.all_to_all(tail_cache, "streams", split_axis=0, concat_axis=0, tiled=True),
        lax.all_to_all(input_cache, "streams", split_axis=0, concat_axis=0, tiled=True),
        lax.all_to_all(resume_slot, "streams", split_axis=0, concat_axis=0, tiled=True),
    )
    arrivals = fetched_slot.shape[0]
    state_steps = fetched_input.shape[1]
    packed = jnp.concatenate(
        [fetched_tail.reshape(arrivals, -1), fetched_input.reshape(arrivals, -1)], axis=1
    )
    one_hot = (fetched_slot[None, :] == jnp.arange(session_rows, dtype=jnp.int32)[:, None]).astype(
        jnp.bfloat16
    )
    placed = jnp.dot(one_hot, packed, preferred_element_type=jnp.float32)
    prev_tail = placed[:, : half_taps * half_width].reshape(session_rows, half_taps, half_width)
    prev_input = (
        placed[:, half_taps * half_width :]
        .reshape(session_rows, state_steps, half_width)
        .astype(jnp.bfloat16)
    )
    upsampled = spread[:, :half_taps] + prev_tail + conv_bias
    new_tail = spread[:, half_taps:].astype(jnp.bfloat16)
    excited = apply_elu(upsampled).astype(jnp.bfloat16)
    window = jnp.concatenate([prev_input, excited], axis=1)
    hidden_width = res_weight.shape[2]
    partial_value = jnp.zeros((session_rows * half_taps, hidden_width), jnp.float32)
    for offset in range(res_weight.shape[0]):
        frames = window[:, offset : offset + half_taps].reshape(
            session_rows * half_taps, half_width
        )
        partial_value = partial_value + jnp.dot(
            frames, res_weight[offset], preferred_element_type=jnp.float32
        )
    partial_value = partial_value.reshape(session_rows, half_taps, hidden_width)
    summed = lax.psum(partial_value, "segment")
    hidden = apply_elu(summed + res_bias).astype(jnp.bfloat16)
    projected = jnp.dot(
        hidden.reshape(session_rows * half_taps, hidden_width),
        skip_weight,
        preferred_element_type=jnp.float32,
    )
    decoded_block = upsampled + projected.reshape(session_rows, half_taps, half_width) + skip_bias
    return (decoded_block.astype(jnp.bfloat16), new_tail)


UNITS = 8
AHEAD = 2
MESH = pl.DeviceIdType.MESH


def elu32(values):
    return jnp.where(values > 0, values, jnp.exp(jnp.minimum(values, 0.0)) - 1.0)


def fused_kernel(
    lat_ref, w_ref, tailc_ref, inpc_ref, slot_hbm, convb_hbm, resw_ref, resb_hbm, skipw_ref, skipb_hbm,
    dec_ref, tail_ref,
    wbuf, lst, exc, pack, cach, spin, tin, outbox, ups, win, resbuf, match, rows_dec, rows_tail,
    slots, convb, resb, skipb,
    w_send, w_recv, x_send, x_recv, l_send, l_recv, sx_send, sx_recv, sy_send, sy_recv,
    half_send, half_recv, c_send, c_recv, win_send, win_recv, out_send, out_recv, sl_sem, local_sem,
):
    g = lax.axis_index("groups")
    j = lax.axis_index("streams")
    c = lax.axis_index("segment")
    z, x = j // 2, lax.rem(j, 2)
    jx = z * 2 + 1 - x
    mine = 2 * g + x
    theirs = 2 * g + 1 - x
    f32, bf16 = jnp.float32, jnp.bfloat16

    def at(gg, jj, cc):
        return {"groups": gg, "streams": jj, "segment": cc}

    def remote(src, dst, ss, rs, dev):
        return pltpu.make_async_remote_copy(
            src_ref=src, dst_ref=dst, send_sem=ss, recv_sem=rs, device_id=dev, device_id_type=MESH
        )

    partner = at(g, j, 1 - c)
    side = at(g, jx, c)
    across = at(1 - g, j, c)
    corner = at(1 - g, jx, c)
    above = at(g, j + 2, c)
    below = at(g, j - 2, c)
    has_up, has_down = z < 3, z > 0

    barrier = pltpu.get_barrier_semaphore()

    def greet(dev):
        pl.semaphore_signal(barrier, inc=1, device_id=dev, device_id_type=MESH)

    greet(side)
    greet(across)
    greet(partner)
    pl.when(has_up)(lambda: greet(above))
    pl.when(has_down)(lambda: greet(below))

    def part(n):
        return slice((n % 2) * 128, (n % 2 + 1) * 128)

    own_w = [
        pltpu.make_async_copy(
            w_ref.at[:, mine, :, part(h)], wbuf.at[:, h, pl.ds(j * 128, 128)], local_sem.at[4 + h]
        )
        for h in range(2)
    ]
    own_res = pltpu.make_async_copy(resw_ref, resbuf.at[c], local_sem.at[1])
    small = [
        pltpu.make_async_copy(slot_hbm, slots, local_sem.at[0]),
        pltpu.make_async_copy(convb_hbm, convb, local_sem.at[2]),
        pltpu.make_async_copy(resb_hbm, resb, local_sem.at[3]),
        pltpu.make_async_copy(skipb_hbm, skipb, local_sem.at[6]),
    ]
    for copy in own_w:
        copy.start()
    own_res.start()
    for copy in small:
        copy.start()
    lst[z] = elu32(lat_ref[...].astype(f32)).astype(bf16).reshape(4, 2, 32, 512)

    pl.semaphore_wait(barrier, 3 + jnp.where(has_up, 1, 0) + jnp.where(has_down, 1, 0))

    def l_copy(s, d, up):
        block = lst.at[z - s if up else z + s, d]
        k = 0 if up else 1
        return remote(block, block, l_send.at[k, s, d], l_recv.at[k, s, d], above if up else below)

    def l_arrival(s, d, up):
        block = lst.at[z - 1 - s if up else z + 1 + s, d]
        k = 0 if up else 1
        return remote(block, block, l_send.at[k, s, d], l_recv.at[k, s, d], below if up else above)

    def share_side(o):
        return remote(lst.at[o, z], exc.at[g, c, :, o, x], sx_send.at[o], sx_recv.at[o], side)

    def share_across(o):
        return remote(lst.at[o, z], exc.at[g, c, :, o, x], sy_send.at[o], sy_recv.at[o], across)

    def share_here(o):
        return pltpu.make_async_copy(lst.at[o, z], exc.at[g, c, :, o, x], sl_sem.at[o])

    def share(o):
        share_side(o).start()
        share_across(o).start()
        share_here(o).start()

    def relay_copy(o):
        block = exc.at[g, c, :, o, 1 - x]
        return remote(block, block, sy_send.at[4 + o], sy_recv.at[4 + o], across)

    def relay(o):
        block = exc.at[g, c, :, o, 1 - x]
        remote(block, block, sx_send.at[o], sx_recv.at[o], side).wait_recv()
        relay_copy(o).start()

    def l_step(s):
        @pl.when(z - 1 - s >= 0)
        def _():
            for d in range(3, s, -1):

                @pl.when(d >= z)
                def _():
                    l_arrival(s, d, True).wait_recv()

                if d >= s + 2:

                    @pl.when(d > z)
                    def _():
                        l_copy(s + 1, d, True).start()

            share(z - 1 - s)

        @pl.when(z + 1 + s <= 3)
        def _():
            for d in range(0, 3 - s):

                @pl.when(d <= z)
                def _():
                    l_arrival(s, d, False).wait_recv()

                if d <= 1 - s:

                    @pl.when(d < z)
                    def _():
                        l_copy(s + 1, d, False).start()

            share(z + 1 + s)

    def relay_step(s):
        pl.when(z - 1 - s >= 0)(lambda: relay(z - 1 - s))
        pl.when(z + 1 + s <= 3)(lambda: relay(z + 1 + s))

    def cross(n):
        return remote(
            w_ref.at[n // 2, theirs, :, part(n)], wbuf.at[n // 2, n % 2, pl.ds(j * 128, 128)], x_send.at[n], x_recv.at[n], side
        )

    def plain(n, up):
        k = 0 if up else 1
        return remote(
            w_ref.at[n // 2, mine, :, part(n)], wbuf.at[n // 2, n % 2, pl.ds(j * 128, 128)], w_send.at[n, k, 0], w_recv.at[n, k, 0],
            above if up else below,
        )

    def crossed(n, up):
        k = 0 if up else 1
        block = wbuf.at[n // 2, n % 2, pl.ds(jx * 128, 128)]
        return remote(block, block, w_send.at[n, k, 1], w_recv.at[n, k, 0], above if up else below)

    def passed(n, s, up):
        k = 0 if up else 1
        block = wbuf.at[n // 2, n % 2, pl.ds((z - s if up else z + s) * 256, 256)]
        return remote(block, block, w_send.at[n, k, 1 + s], w_recv.at[n, k, s], above if up else below)

    def arrival(n, s, up):
        k = 0 if up else 1
        block = wbuf.at[n // 2, n % 2, pl.ds((z - 1 - s if up else z + 1 + s) * 256, 256)]
        return remote(block, block, w_send.at[n, k, 1 + s], w_recv.at[n, k, s], below if up else above)

    def send_plain(n):
        pl.when(has_up)(lambda: plain(n, True).start())
        pl.when(has_down)(lambda: plain(n, False).start())

    def send_crossed(n):
        block = wbuf.at[n // 2, n % 2, pl.ds(jx * 128, 128)]
        remote(block, block, x_send.at[n], x_recv.at[n], side).wait_recv()
        pl.when(has_up)(lambda: crossed(n, True).start())
        pl.when(has_down)(lambda: crossed(n, False).start())

    def forward(n, s):
        @pl.when(z - 1 - s >= 0)
        def _():
            arrival(n, s, True).wait_recv()
            if s < 2:
                pl.when(has_up)(lambda: passed(n, s + 1, True).start())

        @pl.when(z + 1 + s <= 3)
        def _():
            arrival(n, s, False).wait_recv()
            if s < 2:
                pl.when(has_down)(lambda: passed(n, s + 1, False).start())

    def pump(tick):
        for s in (2, 1, 0):
            if 0 <= tick - s < UNITS:
                forward(tick - s, s)
        n = tick + AHEAD
        if n < UNITS:
            send_plain(n)
            send_crossed(n)
        if n + 2 < UNITS:
            cross(n + 2).start()

    for d in (3, 2, 1):
        pl.when(d > z)(lambda d=d: l_copy(0, d, True).start())
    for d in (0, 1, 2):
        pl.when(d < z)(lambda d=d: l_copy(0, d, False).start())
    cross(0).start()
    cross(1).start()
    share(z)
    send_plain(0)
    send_plain(1)
    for n in range(2, AHEAD + 2):
        cross(n).start()
    res_out = remote(resw_ref, resbuf.at[c], half_send.at[2], half_recv.at[2], partner)
    res_in = remote(resw_ref, resbuf.at[1 - c], half_send.at[2], half_recv.at[2], partner)
    res_out.start()

    for copy in small:
        copy.wait()
    for d in range(8):
        pack[d] = jnp.concatenate(
            [
                tailc_ref[d].astype(f32),
                inpc_ref[d].astype(f32),
                jnp.full((6, 256), slots[d].astype(f32)),
            ],
            axis=0,
        ).astype(bf16)

    send_crossed(0)
    send_crossed(1)
    l_step(0)
    relay(z)
    for n in range(2, AHEAD):
        send_plain(n)
        send_crossed(n)
    pump(0)
    l_step(1)
    relay_step(0)
    pump(1)
    l_step(2)
    relay_step(1)
    pump(2)
    relay_step(2)

    def half_copy(gg, index):
        return remote(
            exc.at[gg, c], exc.at[gg, c], half_send.at[index], half_recv.at[index], partner
        )

    def half_arrival(gg, index):
        return remote(
            exc.at[gg, 1 - c], exc.at[gg, 1 - c], half_send.at[index], half_recv.at[index], partner
        )

    for o in range(4):
        share_here(o).wait()
    half_copy(g, 0).start()

    def cache_copy(d):
        peer = lax.rem(j + d, 8)
        return remote(pack.at[peer], cach.at[j], c_send.at[d], c_recv.at[d], at(g, peer, c))

    def cache_arrival(d):
        peer = lax.rem(j + 8 - d, 8)
        return remote(pack.at[0], cach.at[peer], c_send.at[d], c_recv.at[d], at(g, peer, c))

    for d in range(1, 8):
        cache_copy(d).start()
    cach[j] = pack[j]

    for o in range(4):
        for k, xx in ((0, x), (4, 1 - x)):
            block = exc.at[1 - g, c, :, o, xx]
            remote(block, block, sy_send.at[k + o], sy_recv.at[k + o], across).wait_recv()
    half_copy(1 - g, 1).start()
    pump(3)
    for copy in own_w:
        copy.wait()
    half_arrival(g, 0).wait_recv()
    half_arrival(1 - g, 1).wait_recv()

    routes = {1: (g, 1 - x, side), 2: (1 - g, x, across), 3: (1 - g, 1 - x, corner)}

    def out_block(i, lanes, quarter):
        if i < 2:
            return spin.at[4 * i + quarter]
        return tin.at[4 * i - 8 + quarter, :, lanes]

    def out_copy(r, k):
        i, lanes = parts[k]
        gg, xx, dev = routes[r]
        src = outbox.at[r - 1, i] if i < 2 else outbox.at[r - 1, i, :, lanes]
        return remote(src, out_block(i, lanes, mine), out_send.at[r, k], out_recv.at[r, k], dev)

    def out_arrival(r, k):
        i, lanes = parts[k]
        gg, xx, dev = routes[r]
        block = out_block(i, lanes, 2 * gg + xx)
        return remote(block, block, out_send.at[r, k], out_recv.at[r, k], dev)

    whole = slice(0, 256)
    halves = (slice(0, 128), slice(128, 256))
    parts = [(0, whole), (1, whole), (2, halves[0]), (2, halves[1]), (3, halves[0]), (3, halves[1])]

    def spread_of(gg, xx, k):
        i, lanes = parts[k]
        if lanes == whole:
            low = jnp.concatenate([wbuf[i, 0, :512], wbuf[i, 1, :512]], axis=1)
            high = jnp.concatenate([wbuf[i, 0, 512:], wbuf[i, 1, 512:]], axis=1)
        else:
            h = lanes.start // 128
            low, high = wbuf[i, h, :512], wbuf[i, h, 512:]
        value = jnp.dot(exc[gg, 0, xx].reshape(256, 512), low, preferred_element_type=f32)
        value += jnp.dot(exc[gg, 1, xx].reshape(256, 512), high, preferred_element_type=f32)
        return value.astype(bf16)

    def produce(k):
        i, lanes = parts[k]
        for r in (3, 1, 2):
            gg, xx, dev = routes[r]
            outbox[r - 1, i, :, lanes] = spread_of(gg, xx, k)
            out_copy(r, k).start()
        value = spread_of(g, x, k)
        if i < 2:
            spin[4 * i + mine] = value
        else:
            tin[4 * i - 8 + mine, :, lanes] = value

    def placed(row):
        lanes = lax.broadcasted_iota(jnp.int32, (256, 128), 1)
        chosen = jnp.where(lax.rem(lanes, 16) == row, match[...], 0.0).astype(bf16)
        return jnp.dot(chosen, cach[...].reshape(128, 256), preferred_element_type=f32)

    def win_rows(i):
        return pl.ds(0, 6) if i == 0 else pl.ds(6, 4)

    def win_copy(i):
        block = win.at[c, win_rows(i)]
        return remote(block, block, win_send.at[i], win_recv.at[i], partner)

    def win_arrival(i):
        block = win.at[1 - c, win_rows(i)]
        return remote(block, block, win_send.at[i], win_recv.at[i], partner)

    def upsample(i):
        for r in (1, 2, 3):
            out_arrival(r, i).wait_recv()

        @pl.loop(4 * i, 4 * i + 4)
        def _(t):
            value = spin[t].astype(f32) + placed(t) + convb[...]
            ups[t] = value
            win[c, t + 2] = elu32(value).astype(bf16)

        win_copy(i).start()

    def decode(i):
        win_arrival(i).wait_recv()

        @pl.loop(0, 2)
        def _(p):
            t = 4 * i + 2 * p
            branch = jnp.zeros((512, 256), f32) + resb[...]
            for k in range(3):
                for h in range(2):
                    branch = branch + jnp.dot(
                        win[h, pl.ds(t + k, 2)].reshape(512, 256), resbuf[h, k],
                        preferred_element_type=f32,
                    )
            hidden = elu32(branch).astype(bf16)
            value = ups[pl.ds(t, 2)].reshape(512, 256) + jnp.dot(
                hidden, skipw_ref[...], preferred_element_type=f32
            ) + skipb[...]
            for h in range(2):
                rows_dec[h, pl.ds(t, 256, stride=8), :] = value[:256, halves[h]]
                rows_dec[h, pl.ds(t + 1, 256, stride=8), :] = value[256:, halves[h]]

    produce(0)
    pump(4)
    own_res.wait()
    res_in.wait_recv()
    for d in range(1, 8):
        cache_arrival(d).wait_recv()
    named = jnp.broadcast_to(cach[...].astype(f32)[:, 10:11, :], (8, 16, 256)).reshape(128, 256)
    sessions = lax.broadcasted_iota(jnp.int32, (128, 256), 1).astype(f32)
    match[...] = jnp.where(named == sessions, 1.0, 0.0).T
    for i in range(2):
        win[c, i] = placed(8 + i).astype(bf16)
    pump(5)
    produce(1)
    pump(6)
    produce(2)
    pump(7)
    produce(3)
    pump(8)
    produce(4)
    upsample(0)
    pump(9)
    produce(5)
    upsample(1)
    decode(0)
    decode(1)
    for h in range(2):
        dec_ref[:, :, halves[h]] = rows_dec[h].reshape(256, 8, 128).astype(bf16)

    def collect(k):
        i, lanes = parts[k]
        h = lanes.start // 128
        for r in (1, 2, 3):
            out_arrival(r, k).wait_recv()
        for t in range(4 * i - 8, 4 * i - 4):
            rows_tail[h, pl.ds(t, 256, stride=8), :] = tin[t, :, lanes].astype(f32)
        if i == 3:
            tail_ref[:, :, lanes] = rows_tail[h].reshape(256, 8, 128).astype(bf16)

    for k in range(2, 6):
        collect(k)

    for k in range(6):
        for r in (1, 2, 3):
            out_copy(r, k).wait_send()
    for i in range(2):
        win_copy(i).wait_send()
        half_copy((g, 1 - g)[i], i).wait_send()
    res_out.wait_send()
    for d in range(1, 8):
        cache_copy(d).wait_send()
    for o in range(4):
        share_side(o).wait_send()
        share_across(o).wait_send()
        relay_copy(o).wait_send()
    for s in range(3):
        for d in range(4):
            if d >= s + 1:
                pl.when((z - s >= 0) & (d > z))(lambda s=s, d=d: l_copy(s, d, True).wait_send())
            if d <= 2 - s:
                pl.when((z + s <= 3) & (d < z))(lambda s=s, d=d: l_copy(s, d, False).wait_send())

    for n in range(UNITS):
        cross(n).wait_send()
        for up, has in ((True, has_up), (False, has_down)):

            @pl.when(has)
            def _():
                plain(n, up).wait_send()
                crossed(n, up).wait_send()
                for s in (1, 2):
                    pl.when((z - s >= 0) if up else (z + s <= 3))(
                        lambda s=s: passed(n, s, up).wait_send()
                    )


def fused(
    latent, conv_weight, conv_bias, tail_cache, input_cache, resume_slot,
    res_weight, res_bias, skip_weight, skip_bias,
):
    taps_first = conv_weight.transpose(1, 0, 2).reshape(4, 4, 128, 256)
    dma = pltpu.SemaphoreType.DMA
    bf16, f32 = jnp.bfloat16, jnp.float32
    vmem = pl.BlockSpec(memory_space=pltpu.VMEM)
    anywhere = pl.BlockSpec(memory_space=pl.ANY)
    decoded, new_tail = pl.pallas_call(
        fused_kernel,
        out_shape=(
            jax.ShapeDtypeStruct((256, 8, 256), bf16),
            jax.ShapeDtypeStruct((256, 8, 256), bf16),
        ),
        in_specs=[
            vmem, vmem, vmem, vmem, anywhere, anywhere, vmem, anywhere, vmem, anywhere,
        ],
        out_specs=(vmem,) * 2,
        scratch_shapes=[
            pltpu.VMEM((4, 2, 1024, 128), bf16),
            pltpu.VMEM((4, 4, 2, 32, 512), bf16),
            pltpu.VMEM((2, 2, 2, 4, 2, 32, 512), bf16),
            pltpu.VMEM((8, 16, 256), bf16),
            pltpu.VMEM((8, 16, 256), bf16),
            pltpu.VMEM((8, 256, 256), bf16),
            pltpu.VMEM((8, 256, 256), bf16),
            pltpu.VMEM((3, 4, 256, 256), bf16),
            pltpu.VMEM((8, 256, 256), f32),
            pltpu.VMEM((2, 10, 256, 256), bf16),
            pltpu.VMEM((2, 3, 256, 256), bf16),
            pltpu.VMEM((256, 128), f32),
            pltpu.VMEM((2, 2048, 128), f32),
            pltpu.VMEM((2, 2048, 128), f32),
            pltpu.SMEM((8,), jnp.int32),
            pltpu.VMEM((1, 256), f32),
            pltpu.VMEM((1, 256), f32),
            pltpu.VMEM((1, 256), f32),
            dma((8, 2, 4)), dma((8, 2, 3)),
            dma((8,)), dma((8,)),
            dma((2, 3, 4)), dma((2, 3, 4)),
            dma((4,)), dma((4,)),
            dma((8,)), dma((8,)),
            dma((3,)), dma((3,)),
            dma((8,)), dma((8,)),
            dma((2,)), dma((2,)),
            dma((4, 6)), dma((4, 6)),
            dma((4,)), dma((7,)),
        ],
        compiler_params=pltpu.CompilerParams(
            collective_id=0, has_side_effects=True, vmem_limit_bytes=48 * 1024 * 1024
        ),
    )(
        latent, taps_first, tail_cache, input_cache, resume_slot, conv_bias[None, :], res_weight,
        res_bias[None, :], skip_weight, skip_bias[None, :],
    )
    return decoded, new_tail


def solution(mesh):
    sizes = tuple(mesh.shape[name] for name in ("groups", "streams", "segment"))
    body = fused if sizes == (2, 8, 2) else local
    placed = (
        P(("groups", "streams"), "segment"),
        P("streams", None, "segment"),
        P("segment"),
        P(("groups", "streams"), None, "segment"),
        P(("groups", "streams"), None, "segment"),
        P(("groups", "streams")),
        P(None, "segment", None),
        P(),
        P(None, "segment"),
        P("segment"),
    )
    return jax.shard_map(
        body,
        mesh=mesh,
        in_specs=placed,
        out_specs=(
            P(("groups", "streams"), None, "segment"),
            P(("groups", "streams"), None, "segment"),
        ),
        check_vma=False,
    )
```

```python
import jax
import jax.numpy as jnp
from jax import lax
from jax.experimental import pallas as pl
from jax.experimental.pallas import tpu as pltpu
from jax.sharding import PartitionSpec as P


def apply_elu(values):
    return jnp.where(values > 0, values, jnp.expm1(jnp.minimum(values, 0.0)))


def local(
    latent,
    conv_weight,
    conv_bias,
    tail_cache,
    input_cache,
    resume_slot,
    res_weight,
    res_bias,
    skip_weight,
    skip_bias,
):
    handed = lax.all_to_all(latent, "streams", split_axis=0, concat_axis=0, tiled=True)
    excitation_half = apply_elu(handed.astype(jnp.float32)).astype(jnp.bfloat16)
    excitation = lax.all_gather(excitation_half, "segment", axis=1, tiled=True)
    session_rows = excitation.shape[0]
    tap_count = conv_weight.shape[1]
    half_taps = tap_count // 2
    half_width = conv_weight.shape[2]
    piece = lax.all_gather(conv_weight, "streams", axis=0, tiled=True)
    kernel_rows = piece.reshape(piece.shape[0], tap_count * half_width)
    spread = jnp.dot(excitation, kernel_rows, preferred_element_type=jnp.float32)
    spread = spread.reshape(session_rows, tap_count, half_width)
    fetched_tail, fetched_input, fetched_slot = (
        lax.all_to_all(tail_cache, "streams", split_axis=0, concat_axis=0, tiled=True),
        lax.all_to_all(input_cache, "streams", split_axis=0, concat_axis=0, tiled=True),
        lax.all_to_all(resume_slot, "streams", split_axis=0, concat_axis=0, tiled=True),
    )
    arrivals = fetched_slot.shape[0]
    state_steps = fetched_input.shape[1]
    packed = jnp.concatenate(
        [fetched_tail.reshape(arrivals, -1), fetched_input.reshape(arrivals, -1)], axis=1
    )
    one_hot = (fetched_slot[None, :] == jnp.arange(session_rows, dtype=jnp.int32)[:, None]).astype(
        jnp.bfloat16
    )
    placed = jnp.dot(one_hot, packed, preferred_element_type=jnp.float32)
    prev_tail = placed[:, : half_taps * half_width].reshape(session_rows, half_taps, half_width)
    prev_input = (
        placed[:, half_taps * half_width :]
        .reshape(session_rows, state_steps, half_width)
        .astype(jnp.bfloat16)
    )
    upsampled = spread[:, :half_taps] + prev_tail + conv_bias
    new_tail = spread[:, half_taps:].astype(jnp.bfloat16)
    excited = apply_elu(upsampled).astype(jnp.bfloat16)
    window = jnp.concatenate([prev_input, excited], axis=1)
    hidden_width = res_weight.shape[2]
    partial_value = jnp.zeros((session_rows * half_taps, hidden_width), jnp.float32)
    for offset in range(res_weight.shape[0]):
        frames = window[:, offset : offset + half_taps].reshape(
            session_rows * half_taps, half_width
        )
        partial_value = partial_value + jnp.dot(
            frames, res_weight[offset], preferred_element_type=jnp.float32
        )
    partial_value = partial_value.reshape(session_rows, half_taps, hidden_width)
    summed = lax.psum(partial_value, "segment")
    hidden = apply_elu(summed + res_bias).astype(jnp.bfloat16)
    projected = jnp.dot(
        hidden.reshape(session_rows * half_taps, hidden_width),
        skip_weight,
        preferred_element_type=jnp.float32,
    )
    decoded_block = upsampled + projected.reshape(session_rows, half_taps, half_width) + skip_bias
    return (decoded_block.astype(jnp.bfloat16), new_tail)


UNITS = 8
AHEAD = 2
MESH = pl.DeviceIdType.MESH


def elu32(values):
    return jnp.where(values > 0, values, jnp.exp(jnp.minimum(values, 0.0)) - 1.0)


def fused_kernel(
    lat_hbm, w_hbm, tailc_hbm, inpc_hbm, slot_hbm, convb_hbm, resw_hbm, resb_hbm, skipw_hbm, skipb_hbm,
    dec_ref, tail_ref,
    latv, wraw, wide, wside, tailc, inpc, skipw, wbuf, lst, exc, pack, pair, cach, spin, tin, outbox, ups, win, resbuf, match, rows_dec, rows_tail,
    slots, convb, resb, skipb,
    w_send, w_recv, x_send, x_recv, l_send, l_recv, sx_send, sx_recv, sy_send, sy_recv,
    half_send, half_recv, c_send, c_recv, win_send, win_recv, out_send, out_recv, sl_sem, local_sem,
):
    g = lax.axis_index("groups")
    j = lax.axis_index("streams")
    c = lax.axis_index("segment")
    z, x = j // 2, lax.rem(j, 2)
    jx = z * 2 + 1 - x
    mine = 2 * g + x
    theirs = 2 * g + 1 - x
    f32, bf16 = jnp.float32, jnp.bfloat16

    def at(gg, jj, cc):
        return {"groups": gg, "streams": jj, "segment": cc}

    def remote(src, dst, ss, rs, dev):
        return pltpu.make_async_remote_copy(
            src_ref=src, dst_ref=dst, send_sem=ss, recv_sem=rs, device_id=dev, device_id_type=MESH
        )

    partner = at(g, j, 1 - c)
    side = at(g, jx, c)
    across = at(1 - g, j, c)
    corner = at(1 - g, jx, c)
    above = at(g, j + 2, c)
    below = at(g, j - 2, c)
    has_up, has_down = z < 3, z > 0

    barrier = pltpu.get_barrier_semaphore()

    def greet(dev):
        pl.semaphore_signal(barrier, inc=1, device_id=dev, device_id_type=MESH)

    greet(side)
    greet(across)
    greet(partner)
    pl.when(has_up)(lambda: greet(above))
    pl.when(has_down)(lambda: greet(below))

    halves = (slice(0, 128), slice(128, 256))
    own_lat = pltpu.make_async_copy(lat_hbm, latv, local_sem.at[4])
    own_w = pltpu.make_async_copy(w_hbm, wraw, local_sem.at[5])
    own_res = pltpu.make_async_copy(resw_hbm, resbuf.at[c], local_sem.at[1])
    small = [
        pltpu.make_async_copy(tailc_hbm, tailc, local_sem.at[7]),
        pltpu.make_async_copy(inpc_hbm, inpc, local_sem.at[8]),
        pltpu.make_async_copy(skipw_hbm, skipw, local_sem.at[9]),
        pltpu.make_async_copy(slot_hbm, slots, local_sem.at[0]),
        pltpu.make_async_copy(convb_hbm, convb, local_sem.at[2]),
        pltpu.make_async_copy(resb_hbm, resb, local_sem.at[3]),
        pltpu.make_async_copy(skipb_hbm, skipb, local_sem.at[6]),
    ]
    own_lat.start()
    own_w.start()
    own_res.start()
    for copy in small:
        copy.start()

    def regroup(i):
        for quarter in (theirs, mine):
            for h in range(2):
                block = wide[h, pl.ds(4 * i + quarter, 128, stride=16), :].astype(bf16)
                if quarter is theirs:
                    wside[2 * i + h] = block
                else:
                    wbuf[i, h, pl.ds(j * 128, 128)] = block

    own_lat.wait()
    lst[z] = elu32(latv[...].astype(f32)).astype(bf16).reshape(4, 2, 32, 512)

    pl.semaphore_wait(barrier, 3 + jnp.where(has_up, 1, 0) + jnp.where(has_down, 1, 0))

    def l_copy(s, d, up):
        block = lst.at[z - s if up else z + s, d]
        k = 0 if up else 1
        return remote(block, block, l_send.at[k, s, d], l_recv.at[k, s, d], above if up else below)

    def l_arrival(s, d, up):
        block = lst.at[z - 1 - s if up else z + 1 + s, d]
        k = 0 if up else 1
        return remote(block, block, l_send.at[k, s, d], l_recv.at[k, s, d], below if up else above)

    def share_side(o):
        return remote(lst.at[o, z], exc.at[g, c, :, o, x], sx_send.at[o], sx_recv.at[o], side)

    def share_across(o):
        return remote(lst.at[o, z], exc.at[g, c, :, o, x], sy_send.at[o], sy_recv.at[o], across)

    def share_here(o):
        return pltpu.make_async_copy(lst.at[o, z], exc.at[g, c, :, o, x], sl_sem.at[o])

    def share(o):
        share_side(o).start()
        share_across(o).start()
        share_here(o).start()

    def relay_copy(o):
        block = exc.at[g, c, :, o, 1 - x]
        return remote(block, block, sy_send.at[4 + o], sy_recv.at[4 + o], across)

    def relay(o):
        block = exc.at[g, c, :, o, 1 - x]
        remote(block, block, sx_send.at[o], sx_recv.at[o], side).wait_recv()
        relay_copy(o).start()

    def l_step(s):
        @pl.when(z - 1 - s >= 0)
        def _():
            for d in range(3, s, -1):

                @pl.when(d >= z)
                def _():
                    l_arrival(s, d, True).wait_recv()

                if d >= s + 2:

                    @pl.when(d > z)
                    def _():
                        l_copy(s + 1, d, True).start()

            share(z - 1 - s)

        @pl.when(z + 1 + s <= 3)
        def _():
            for d in range(0, 3 - s):

                @pl.when(d <= z)
                def _():
                    l_arrival(s, d, False).wait_recv()

                if d <= 1 - s:

                    @pl.when(d < z)
                    def _():
                        l_copy(s + 1, d, False).start()

            share(z + 1 + s)

    def relay_step(s):
        pl.when(z - 1 - s >= 0)(lambda: relay(z - 1 - s))
        pl.when(z + 1 + s <= 3)(lambda: relay(z + 1 + s))

    def cross(n):
        return remote(
            wside.at[n], wbuf.at[n // 2, n % 2, pl.ds(j * 128, 128)], x_send.at[n], x_recv.at[n], side
        )

    def plain(n, up):
        k = 0 if up else 1
        block = wbuf.at[n // 2, n % 2, pl.ds(j * 128, 128)]
        return remote(
            block, block, w_send.at[n, k, 0], w_recv.at[n, k, 0], above if up else below
        )

    def crossed(n, up):
        k = 0 if up else 1
        block = wbuf.at[n // 2, n % 2, pl.ds(jx * 128, 128)]
        return remote(block, block, w_send.at[n, k, 1], w_recv.at[n, k, 0], above if up else below)

    def passed(n, s, up):
        k = 0 if up else 1
        block = wbuf.at[n // 2, n % 2, pl.ds((z - s if up else z + s) * 256, 256)]
        return remote(block, block, w_send.at[n, k, 1 + s], w_recv.at[n, k, s], above if up else below)

    def arrival(n, s, up):
        k = 0 if up else 1
        block = wbuf.at[n // 2, n % 2, pl.ds((z - 1 - s if up else z + 1 + s) * 256, 256)]
        return remote(block, block, w_send.at[n, k, 1 + s], w_recv.at[n, k, s], below if up else above)

    def send_plain(n):
        pl.when(has_up)(lambda: plain(n, True).start())
        pl.when(has_down)(lambda: plain(n, False).start())

    def send_crossed(n):
        block = wbuf.at[n // 2, n % 2, pl.ds(jx * 128, 128)]
        remote(block, block, x_send.at[n], x_recv.at[n], side).wait_recv()
        pl.when(has_up)(lambda: crossed(n, True).start())
        pl.when(has_down)(lambda: crossed(n, False).start())

    def forward(n, s):
        @pl.when(z - 1 - s >= 0)
        def _():
            arrival(n, s, True).wait_recv()
            if s < 2:
                pl.when(has_up)(lambda: passed(n, s + 1, True).start())

        @pl.when(z + 1 + s <= 3)
        def _():
            arrival(n, s, False).wait_recv()
            if s < 2:
                pl.when(has_down)(lambda: passed(n, s + 1, False).start())

    def pump(tick):
        for s in (2, 1, 0):
            if 0 <= tick - s < UNITS:
                forward(tick - s, s)
        n = tick + AHEAD
        if n < UNITS:
            send_plain(n)
            send_crossed(n)
        if n + 2 < UNITS:
            cross(n + 2).start()

    for d in (3, 2, 1):
        pl.when(d > z)(lambda d=d: l_copy(0, d, True).start())
    for d in (0, 1, 2):
        pl.when(d < z)(lambda d=d: l_copy(0, d, False).start())
    share(z)
    own_w.wait()
    for h in range(2):
        wide[h] = wraw[:, :, halves[h]].reshape(2048, 128).astype(f32)
    regroup(0)
    cross(0).start()
    cross(1).start()
    send_plain(0)
    for i in range(1, 4):
        regroup(i)
    for n in range(2, AHEAD + 2):
        cross(n).start()
    own_res.wait()
    res_out = remote(resbuf.at[c], resbuf.at[c], half_send.at[2], half_recv.at[2], partner)
    res_in = remote(resbuf.at[c], resbuf.at[1 - c], half_send.at[2], half_recv.at[2], partner)
    res_out.start()

    for copy in small:
        copy.wait()
    for d in range(8):
        pack[d % 2, d // 2] = jnp.concatenate(
            [
                tailc[d].astype(f32),
                inpc[d].astype(f32),
                jnp.full((6, 256), slots[d].astype(f32)),
            ],
            axis=0,
        ).astype(bf16)

    swap_out = remote(pack.at[1 - x], pair.at[:, x], c_send.at[0], c_recv.at[0], side)
    swap_in = remote(pack.at[1 - x], pair.at[:, 1 - x], c_send.at[0], c_recv.at[0], side)
    swap_out.start()
    pair[:, x] = pack[x]

    send_crossed(0)
    send_plain(1)
    send_crossed(1)
    l_step(0)
    relay(z)
    for n in range(2, AHEAD):
        send_plain(n)
        send_crossed(n)
    pump(0)
    l_step(1)
    relay_step(0)
    pump(1)
    l_step(2)
    relay_step(1)
    pump(2)
    relay_step(2)

    def half_copy(gg, index):
        return remote(
            exc.at[gg, c], exc.at[gg, c], half_send.at[index], half_recv.at[index], partner
        )

    def half_arrival(gg, index):
        return remote(
            exc.at[gg, 1 - c], exc.at[gg, 1 - c], half_send.at[index], half_recv.at[index], partner
        )

    for o in range(4):
        share_here(o).wait()
    half_copy(g, 0).start()

    def cache_copy(d):
        peer = lax.rem(z + d, 4)
        return remote(pair.at[peer], cach.at[z], c_send.at[d], c_recv.at[d], at(g, peer * 2 + x, c))

    def cache_arrival(d):
        peer = lax.rem(z + 4 - d, 4)
        return remote(pair.at[0], cach.at[peer], c_send.at[d], c_recv.at[d], at(g, peer * 2 + x, c))

    swap_in.wait_recv()
    for d in range(1, 4):
        cache_copy(d).start()
    cach[z] = pair[z]

    for o in range(4):
        for k, xx in ((0, x), (4, 1 - x)):
            block = exc.at[1 - g, c, :, o, xx]
            remote(block, block, sy_send.at[k + o], sy_recv.at[k + o], across).wait_recv()
    half_copy(1 - g, 1).start()
    pump(3)
    half_arrival(g, 0).wait_recv()
    half_arrival(1 - g, 1).wait_recv()

    routes = {1: (g, 1 - x, side), 2: (1 - g, x, across), 3: (1 - g, 1 - x, corner)}

    def out_block(i, lanes, quarter):
        if i < 2:
            return spin.at[4 * i + quarter]
        return tin.at[4 * i - 8 + quarter, :, lanes]

    def out_copy(r, k):
        i, lanes = parts[k]
        gg, xx, dev = routes[r]
        src = outbox.at[r - 1, i] if i < 2 else outbox.at[r - 1, i, :, lanes]
        return remote(src, out_block(i, lanes, mine), out_send.at[r, k], out_recv.at[r, k], dev)

    def out_arrival(r, k):
        i, lanes = parts[k]
        gg, xx, dev = routes[r]
        block = out_block(i, lanes, 2 * gg + xx)
        return remote(block, block, out_send.at[r, k], out_recv.at[r, k], dev)

    whole = slice(0, 256)
    parts = [(0, whole), (1, whole), (2, halves[0]), (2, halves[1]), (3, halves[0]), (3, halves[1])]

    def spread_of(gg, xx, k):
        i, lanes = parts[k]
        if lanes == whole:
            low = jnp.concatenate([wbuf[i, 0, :512], wbuf[i, 1, :512]], axis=1)
            high = jnp.concatenate([wbuf[i, 0, 512:], wbuf[i, 1, 512:]], axis=1)
        else:
            h = lanes.start // 128
            low, high = wbuf[i, h, :512], wbuf[i, h, 512:]
        value = jnp.dot(exc[gg, 0, xx].reshape(256, 512), low, preferred_element_type=f32)
        value += jnp.dot(exc[gg, 1, xx].reshape(256, 512), high, preferred_element_type=f32)
        return value.astype(bf16)

    def produce(k):
        i, lanes = parts[k]
        for r in (3, 1, 2):
            gg, xx, dev = routes[r]
            outbox[r - 1, i, :, lanes] = spread_of(gg, xx, k)
            out_copy(r, k).start()
        value = spread_of(g, x, k)
        if i < 2:
            spin[4 * i + mine] = value
        else:
            tin[4 * i - 8 + mine, :, lanes] = value

    def placed(row):
        lanes = lax.broadcasted_iota(jnp.int32, (256, 128), 1)
        chosen = jnp.where(lax.rem(lanes, 16) == row, match[...], 0.0).astype(bf16)
        return jnp.dot(chosen, cach[...].reshape(128, 256), preferred_element_type=f32)

    def win_rows(i):
        return pl.ds(0, 6) if i == 0 else pl.ds(6, 4)

    def win_copy(i):
        block = win.at[c, win_rows(i)]
        return remote(block, block, win_send.at[i], win_recv.at[i], partner)

    def win_arrival(i):
        block = win.at[1 - c, win_rows(i)]
        return remote(block, block, win_send.at[i], win_recv.at[i], partner)

    def upsample(i):
        for r in (1, 2, 3):
            out_arrival(r, i).wait_recv()

        @pl.loop(4 * i, 4 * i + 4)
        def _(t):
            value = spin[t].astype(f32) + placed(t) + convb[...]
            ups[t] = value
            win[c, t + 2] = elu32(value).astype(bf16)

        win_copy(i).start()

    def decode(i):
        win_arrival(i).wait_recv()

        @pl.loop(0, 2)
        def _(p):
            t = 4 * i + 2 * p
            branch = jnp.zeros((512, 256), f32) + resb[...]
            for k in range(3):
                for h in range(2):
                    branch = branch + jnp.dot(
                        win[h, pl.ds(t + k, 2)].reshape(512, 256), resbuf[h, k],
                        preferred_element_type=f32,
                    )
            hidden = elu32(branch).astype(bf16)
            value = ups[pl.ds(t, 2)].reshape(512, 256) + jnp.dot(
                hidden, skipw[...], preferred_element_type=f32
            ) + skipb[...]
            for h in range(2):
                rows_dec[h, pl.ds(t, 256, stride=8), :] = value[:256, halves[h]]
                rows_dec[h, pl.ds(t + 1, 256, stride=8), :] = value[256:, halves[h]]

    produce(0)
    pump(4)
    res_in.wait_recv()
    for d in range(1, 4):
        cache_arrival(d).wait_recv()
    named = jnp.broadcast_to(cach[...].reshape(8, 16, 256).astype(f32)[:, 10:11, :], (8, 16, 256)).reshape(128, 256)
    sessions = lax.broadcasted_iota(jnp.int32, (128, 256), 1).astype(f32)
    match[...] = jnp.where(named == sessions, 1.0, 0.0).T
    for i in range(2):
        win[c, i] = placed(8 + i).astype(bf16)
    pump(5)
    produce(1)
    pump(6)
    produce(2)
    pump(7)
    produce(3)
    pump(8)
    produce(4)
    upsample(0)
    pump(9)
    produce(5)
    upsample(1)
    decode(0)
    decode(1)
    for h in range(2):
        dec_ref[:, :, halves[h]] = rows_dec[h].reshape(256, 8, 128).astype(bf16)

    def collect(k):
        i, lanes = parts[k]
        h = lanes.start // 128
        for r in (1, 2, 3):
            out_arrival(r, k).wait_recv()
        for t in range(4 * i - 8, 4 * i - 4):
            rows_tail[h, pl.ds(t, 256, stride=8), :] = tin[t, :, lanes].astype(f32)
        if i == 3:
            tail_ref[:, :, lanes] = rows_tail[h].reshape(256, 8, 128).astype(bf16)

    for k in range(2, 6):
        collect(k)

    for k in range(6):
        for r in (1, 2, 3):
            out_copy(r, k).wait_send()
    for i in range(2):
        win_copy(i).wait_send()
        half_copy((g, 1 - g)[i], i).wait_send()
    res_out.wait_send()
    swap_out.wait_send()
    for d in range(1, 4):
        cache_copy(d).wait_send()
    for o in range(4):
        share_side(o).wait_send()
        share_across(o).wait_send()
        relay_copy(o).wait_send()
    for s in range(3):
        for d in range(4):
            if d >= s + 1:
                pl.when((z - s >= 0) & (d > z))(lambda s=s, d=d: l_copy(s, d, True).wait_send())
            if d <= 2 - s:
                pl.when((z + s <= 3) & (d < z))(lambda s=s, d=d: l_copy(s, d, False).wait_send())

    for n in range(UNITS):
        cross(n).wait_send()
        for up, has in ((True, has_up), (False, has_down)):

            @pl.when(has)
            def _():
                plain(n, up).wait_send()
                crossed(n, up).wait_send()
                for s in (1, 2):
                    pl.when((z - s >= 0) if up else (z + s <= 3))(
                        lambda s=s: passed(n, s, up).wait_send()
                    )


def publish(dec_ref, tail_ref, dec_out, tail_out, sem):
    copies = (
        pltpu.make_async_copy(dec_ref, dec_out, sem.at[0]),
        pltpu.make_async_copy(tail_ref, tail_out, sem.at[1]),
    )
    for copy in copies:
        copy.start()
    for copy in copies:
        copy.wait()


def fused(
    latent, conv_weight, conv_bias, tail_cache, input_cache, resume_slot,
    res_weight, res_bias, skip_weight, skip_bias,
):
    dma = pltpu.SemaphoreType.DMA
    bf16, f32 = jnp.bfloat16, jnp.float32
    vmem = pl.BlockSpec(memory_space=pltpu.VMEM)
    anywhere = pl.BlockSpec(memory_space=pl.ANY)
    operands = [
        pltpu.with_memory_space_constraint(array, pltpu.HBM)
        for array in (
            latent, conv_weight, tail_cache, input_cache, resume_slot, conv_bias[None, :], res_weight,
            res_bias[None, :], skip_weight, skip_bias[None, :],
        )
    ]
    decoded, new_tail = pl.pallas_call(
        fused_kernel,
        out_shape=(
            jax.ShapeDtypeStruct((256, 8, 256), bf16),
            jax.ShapeDtypeStruct((256, 8, 256), bf16),
        ),
        in_specs=[anywhere] * 10,
        out_specs=(vmem,) * 2,
        scratch_shapes=[
            pltpu.VMEM((256, 512), bf16),
            pltpu.VMEM((128, 16, 256), bf16),
            pltpu.VMEM((2, 2048, 128), f32),
            pltpu.VMEM((8, 128, 128), bf16),
            pltpu.VMEM((8, 8, 256), bf16),
            pltpu.VMEM((8, 2, 256), bf16),
            pltpu.VMEM((256, 256), bf16),
            pltpu.VMEM((4, 2, 1024, 128), bf16),
            pltpu.VMEM((4, 4, 2, 32, 512), bf16),
            pltpu.VMEM((2, 2, 2, 4, 2, 32, 512), bf16),
            pltpu.VMEM((2, 4, 16, 256), bf16),
            pltpu.VMEM((4, 2, 16, 256), bf16),
            pltpu.VMEM((4, 2, 16, 256), bf16),
            pltpu.VMEM((8, 256, 256), bf16),
            pltpu.VMEM((8, 256, 256), bf16),
            pltpu.VMEM((3, 4, 256, 256), bf16),
            pltpu.VMEM((8, 256, 256), f32),
            pltpu.VMEM((2, 10, 256, 256), bf16),
            pltpu.VMEM((2, 3, 256, 256), bf16),
            pltpu.VMEM((256, 128), f32),
            pltpu.VMEM((2, 2048, 128), f32),
            pltpu.VMEM((2, 2048, 128), f32),
            pltpu.SMEM((8,), jnp.int32),
            pltpu.VMEM((1, 256), f32),
            pltpu.VMEM((1, 256), f32),
            pltpu.VMEM((1, 256), f32),
            dma((8, 2, 4)), dma((8, 2, 3)),
            dma((8,)), dma((8,)),
            dma((2, 3, 4)), dma((2, 3, 4)),
            dma((4,)), dma((4,)),
            dma((8,)), dma((8,)),
            dma((3,)), dma((3,)),
            dma((8,)), dma((8,)),
            dma((2,)), dma((2,)),
            dma((4, 6)), dma((4, 6)),
            dma((4,)), dma((10,)),
        ],
        compiler_params=pltpu.CompilerParams(
            collective_id=0, has_side_effects=True, vmem_limit_bytes=48 * 1024 * 1024
        ),
    )(*operands)
    return pl.pallas_call(
        publish,
        out_shape=(
            jax.ShapeDtypeStruct((256, 8, 256), bf16),
            jax.ShapeDtypeStruct((256, 8, 256), bf16),
        ),
        in_specs=[vmem] * 2,
        out_specs=(anywhere,) * 2,
        scratch_shapes=[dma((2,))],
    )(*[pltpu.with_memory_space_constraint(array, pltpu.VMEM) for array in (decoded, new_tail)])


def solution(mesh):
    sizes = tuple(mesh.shape[name] for name in ("groups", "streams", "segment"))
    body = fused if sizes == (2, 8, 2) else local
    placed = (
        P(("groups", "streams"), "segment"),
        P("streams", None, "segment"),
        P("segment"),
        P(("groups", "streams"), None, "segment"),
        P(("groups", "streams"), None, "segment"),
        P(("groups", "streams")),
        P(None, "segment", None),
        P(),
        P(None, "segment"),
        P("segment"),
    )
    return jax.shard_map(
        body,
        mesh=mesh,
        in_specs=placed,
        out_specs=(
            P(("groups", "streams"), None, "segment"),
            P(("groups", "streams"), None, "segment"),
        ),
        check_vma=False,
    )
```

```python
import jax
import jax.numpy as jnp
from jax import lax
from jax.experimental import pallas as pl
from jax.experimental.pallas import tpu as pltpu
from jax.sharding import PartitionSpec as P


def apply_elu(values):
    return jnp.where(values > 0, values, jnp.expm1(jnp.minimum(values, 0.0)))


def local(
    latent,
    conv_weight,
    conv_bias,
    tail_cache,
    input_cache,
    resume_slot,
    res_weight,
    res_bias,
    skip_weight,
    skip_bias,
):
    handed = lax.all_to_all(latent, "streams", split_axis=0, concat_axis=0, tiled=True)
    excitation_half = apply_elu(handed.astype(jnp.float32)).astype(jnp.bfloat16)
    excitation = lax.all_gather(excitation_half, "segment", axis=1, tiled=True)
    session_rows = excitation.shape[0]
    tap_count = conv_weight.shape[1]
    half_taps = tap_count // 2
    half_width = conv_weight.shape[2]
    piece = lax.all_gather(conv_weight, "streams", axis=0, tiled=True)
    kernel_rows = piece.reshape(piece.shape[0], tap_count * half_width)
    spread = jnp.dot(excitation, kernel_rows, preferred_element_type=jnp.float32)
    spread = spread.reshape(session_rows, tap_count, half_width)
    fetched_tail, fetched_input, fetched_slot = (
        lax.all_to_all(tail_cache, "streams", split_axis=0, concat_axis=0, tiled=True),
        lax.all_to_all(input_cache, "streams", split_axis=0, concat_axis=0, tiled=True),
        lax.all_to_all(resume_slot, "streams", split_axis=0, concat_axis=0, tiled=True),
    )
    arrivals = fetched_slot.shape[0]
    state_steps = fetched_input.shape[1]
    packed = jnp.concatenate(
        [fetched_tail.reshape(arrivals, -1), fetched_input.reshape(arrivals, -1)], axis=1
    )
    one_hot = (fetched_slot[None, :] == jnp.arange(session_rows, dtype=jnp.int32)[:, None]).astype(
        jnp.bfloat16
    )
    placed = jnp.dot(one_hot, packed, preferred_element_type=jnp.float32)
    prev_tail = placed[:, : half_taps * half_width].reshape(session_rows, half_taps, half_width)
    prev_input = (
        placed[:, half_taps * half_width :]
        .reshape(session_rows, state_steps, half_width)
        .astype(jnp.bfloat16)
    )
    upsampled = spread[:, :half_taps] + prev_tail + conv_bias
    new_tail = spread[:, half_taps:].astype(jnp.bfloat16)
    excited = apply_elu(upsampled).astype(jnp.bfloat16)
    window = jnp.concatenate([prev_input, excited], axis=1)
    hidden_width = res_weight.shape[2]
    partial_value = jnp.zeros((session_rows * half_taps, hidden_width), jnp.float32)
    for offset in range(res_weight.shape[0]):
        frames = window[:, offset : offset + half_taps].reshape(
            session_rows * half_taps, half_width
        )
        partial_value = partial_value + jnp.dot(
            frames, res_weight[offset], preferred_element_type=jnp.float32
        )
    partial_value = partial_value.reshape(session_rows, half_taps, hidden_width)
    summed = lax.psum(partial_value, "segment")
    hidden = apply_elu(summed + res_bias).astype(jnp.bfloat16)
    projected = jnp.dot(
        hidden.reshape(session_rows * half_taps, hidden_width),
        skip_weight,
        preferred_element_type=jnp.float32,
    )
    decoded_block = upsampled + projected.reshape(session_rows, half_taps, half_width) + skip_bias
    return (decoded_block.astype(jnp.bfloat16), new_tail)


UNITS = 8
AHEAD = 2
MESH = pl.DeviceIdType.MESH


def elu32(values):
    return jnp.where(values > 0, values, jnp.exp(jnp.minimum(values, 0.0)) - 1.0)


def fused_kernel(
    lat_hbm, w_hbm, tailc_hbm, inpc_hbm, slot_hbm, convb_hbm, resw_hbm, resb_hbm, skipw_hbm, skipb_hbm,
    dec_ref, tail_ref,
    latv, wraw, wide, wside, tailc, inpc, skipw, wbuf, lst, exc, pack, pair, cach, spin, tin, outbox, ups, win, resbuf, match, rows_dec, rows_tail,
    slots, convb, resb, skipb,
    w_send, w_recv, x_send, x_recv, l_send, l_recv, sx_send, sx_recv, sy_send, sy_recv,
    half_send, half_recv, c_send, c_recv, win_send, win_recv, out_send, out_recv, sl_sem, local_sem, news,
):
    g = lax.axis_index("groups")
    j = lax.axis_index("streams")
    c = lax.axis_index("segment")
    z, x = j // 2, lax.rem(j, 2)
    jx = z * 2 + 1 - x
    mine = 2 * g + x
    theirs = 2 * g + 1 - x
    f32, bf16 = jnp.float32, jnp.bfloat16

    def at(gg, jj, cc):
        return {"groups": gg, "streams": jj, "segment": cc}

    def remote(src, dst, ss, rs, dev):
        return pltpu.make_async_remote_copy(
            src_ref=src, dst_ref=dst, send_sem=ss, recv_sem=rs, device_id=dev, device_id_type=MESH
        )

    partner = at(g, j, 1 - c)
    side = at(g, jx, c)
    across = at(1 - g, j, c)
    corner = at(1 - g, jx, c)
    above = at(g, j + 2, c)
    below = at(g, j - 2, c)
    has_up, has_down = z < 3, z > 0

    barrier = pltpu.get_barrier_semaphore()

    def greet(dev):
        pl.semaphore_signal(barrier, inc=1, device_id=dev, device_id_type=MESH)

    greet(side)
    greet(across)
    greet(partner)
    pl.when(has_up)(lambda: greet(above))
    pl.when(has_down)(lambda: greet(below))

    halves = (slice(0, 128), slice(128, 256))
    own_lat = pltpu.make_async_copy(lat_hbm, latv, local_sem.at[4])
    own_w = pltpu.make_async_copy(w_hbm, wraw, local_sem.at[5])
    own_res = pltpu.make_async_copy(resw_hbm, resbuf.at[c], local_sem.at[1])
    small = [
        pltpu.make_async_copy(tailc_hbm, tailc, local_sem.at[7]),
        pltpu.make_async_copy(inpc_hbm, inpc, local_sem.at[8]),
        pltpu.make_async_copy(skipw_hbm, skipw, local_sem.at[9]),
        pltpu.make_async_copy(slot_hbm, slots, local_sem.at[0]),
        pltpu.make_async_copy(convb_hbm, convb, local_sem.at[2]),
        pltpu.make_async_copy(resb_hbm, resb, local_sem.at[3]),
        pltpu.make_async_copy(skipb_hbm, skipb, local_sem.at[6]),
    ]
    own_lat.start()
    own_w.start()
    own_res.start()
    for copy in small:
        copy.start()

    def regroup(i):
        for quarter in (theirs, mine):
            for h in range(2):
                block = wide[h, pl.ds(4 * i + quarter, 128, stride=16), :].astype(bf16)
                if quarter is theirs:
                    wside[2 * i + h] = block
                else:
                    wbuf[i, h, pl.ds(j * 128, 128)] = block

    own_lat.wait()
    lst[z] = elu32(latv[...].astype(f32)).astype(bf16).reshape(4, 2, 32, 512)

    pl.semaphore_wait(barrier, 3 + jnp.where(has_up, 1, 0) + jnp.where(has_down, 1, 0))

    def line(zz):
        return at(g, zz * 2 + x, c)

    def l_copy(hops, up):
        d = z + hops if up else z - hops
        return remote(lst.at[z, d], lst.at[z, d], l_send.at[d], l_recv.at[z], line(d))

    def l_arrival(o):
        return remote(lst.at[o, z], lst.at[o, z], l_send.at[o], l_recv.at[o], line(o))

    def l_send_out(hops):
        pl.when(z + hops <= 3)(lambda: l_copy(hops, True).start())
        pl.when(z - hops >= 0)(lambda: l_copy(hops, False).start())

    def tell(index, dev):
        pl.semaphore_signal(news.at[index], inc=1, device_id=dev, device_id_type=MESH)

    def tell_second():
        @pl.when((z > 0) & (z < 3))
        def _():
            tell(0, below)
            tell(1, above)

    def hear_second():
        pl.when(z <= 1)(lambda: pl.semaphore_wait(news.at[0], 1))
        pl.when(z >= 2)(lambda: pl.semaphore_wait(news.at[1], 1))
        pl.when(z == 1)(lambda: tell(2, below))
        pl.when(z == 2)(lambda: tell(3, above))

    def hear_third():
        pl.when(z == 0)(lambda: pl.semaphore_wait(news.at[2], 1))
        pl.when(z == 3)(lambda: pl.semaphore_wait(news.at[3], 1))

    def share_side(o):
        return remote(lst.at[o, z], exc.at[g, c, :, o, x], sx_send.at[o], sx_recv.at[o], side)

    def share_across(o):
        return remote(lst.at[o, z], exc.at[g, c, :, o, x], sy_send.at[o], sy_recv.at[o], across)

    def share_here(o):
        return pltpu.make_async_copy(lst.at[o, z], exc.at[g, c, :, o, x], sl_sem.at[o])

    def share(o):
        share_side(o).start()
        share_across(o).start()
        share_here(o).start()

    def relay_copy(o):
        block = exc.at[g, c, :, o, 1 - x]
        return remote(block, block, sy_send.at[4 + o], sy_recv.at[4 + o], across)

    def relay(o):
        block = exc.at[g, c, :, o, 1 - x]
        remote(block, block, sx_send.at[o], sx_recv.at[o], side).wait_recv()
        relay_copy(o).start()

    def l_step(s):
        for o, there in ((z - 1 - s, z - 1 - s >= 0), (z + 1 + s, z + 1 + s <= 3)):

            @pl.when(there)
            def _():
                l_arrival(o).wait_recv()
                share(o)

    def relay_step(s):
        pl.when(z - 1 - s >= 0)(lambda: relay(z - 1 - s))
        pl.when(z + 1 + s <= 3)(lambda: relay(z + 1 + s))

    def cross(n):
        return remote(
            wside.at[n], wbuf.at[n // 2, n % 2, pl.ds(j * 128, 128)], x_send.at[n], x_recv.at[n], side
        )

    def plain(n, up):
        k = 0 if up else 1
        block = wbuf.at[n // 2, n % 2, pl.ds(j * 128, 128)]
        return remote(
            block, block, w_send.at[n, k, 0], w_recv.at[n, k, 0], above if up else below
        )

    def crossed(n, up):
        k = 0 if up else 1
        block = wbuf.at[n // 2, n % 2, pl.ds(jx * 128, 128)]
        return remote(block, block, w_send.at[n, k, 1], w_recv.at[n, k, 0], above if up else below)

    def passed(n, s, up):
        k = 0 if up else 1
        block = wbuf.at[n // 2, n % 2, pl.ds((z - s if up else z + s) * 256, 256)]
        return remote(block, block, w_send.at[n, k, 1 + s], w_recv.at[n, k, s], above if up else below)

    def arrival(n, s, up):
        k = 0 if up else 1
        block = wbuf.at[n // 2, n % 2, pl.ds((z - 1 - s if up else z + 1 + s) * 256, 256)]
        return remote(block, block, w_send.at[n, k, 1 + s], w_recv.at[n, k, s], below if up else above)

    def send_plain(n):
        pl.when(has_up)(lambda: plain(n, True).start())
        pl.when(has_down)(lambda: plain(n, False).start())

    def send_crossed(n):
        block = wbuf.at[n // 2, n % 2, pl.ds(jx * 128, 128)]
        remote(block, block, x_send.at[n], x_recv.at[n], side).wait_recv()
        pl.when(has_up)(lambda: crossed(n, True).start())
        pl.when(has_down)(lambda: crossed(n, False).start())

    def forward(n, s):
        @pl.when(z - 1 - s >= 0)
        def _():
            arrival(n, s, True).wait_recv()
            if s < 2:
                pl.when(has_up)(lambda: passed(n, s + 1, True).start())

        @pl.when(z + 1 + s <= 3)
        def _():
            arrival(n, s, False).wait_recv()
            if s < 2:
                pl.when(has_down)(lambda: passed(n, s + 1, False).start())

    def pump(tick):
        for s in (2, 1, 0):
            if 0 <= tick - s < UNITS:
                forward(tick - s, s)
        n = tick + AHEAD
        if n < UNITS:
            send_plain(n)
            send_crossed(n)
        if n + 2 < UNITS:
            cross(n + 2).start()

    l_send_out(1)
    tell_second()
    share(z)
    own_w.wait()
    for h in range(2):
        wide[h] = wraw[:, :, halves[h]].reshape(2048, 128).astype(f32)
    regroup(0)
    cross(0).start()
    cross(1).start()
    send_plain(0)
    hear_second()
    l_send_out(2)
    for i in range(1, 4):
        regroup(i)
    hear_third()
    l_send_out(3)
    for n in range(2, AHEAD + 2):
        cross(n).start()
    own_res.wait()
    res_out = remote(resbuf.at[c], resbuf.at[c], half_send.at[2], half_recv.at[2], partner)
    res_in = remote(resbuf.at[c], resbuf.at[1 - c], half_send.at[2], half_recv.at[2], partner)
    res_out.start()

    for copy in small:
        copy.wait()
    for d in range(8):
        pack[d % 2, d // 2] = jnp.concatenate(
            [
                tailc[d].astype(f32),
                inpc[d].astype(f32),
                jnp.full((6, 256), slots[d].astype(f32)),
            ],
            axis=0,
        ).astype(bf16)

    swap_out = remote(pack.at[1 - x], pair.at[:, x], c_send.at[0], c_recv.at[0], side)
    swap_in = remote(pack.at[1 - x], pair.at[:, 1 - x], c_send.at[0], c_recv.at[0], side)
    swap_out.start()
    pair[:, x] = pack[x]

    send_crossed(0)
    send_plain(1)
    send_crossed(1)
    l_step(0)
    relay(z)
    for n in range(2, AHEAD):
        send_plain(n)
        send_crossed(n)
    pump(0)
    l_step(1)
    relay_step(0)
    pump(1)
    l_step(2)
    relay_step(1)
    pump(2)
    relay_step(2)

    def half_copy(gg, index):
        return remote(
            exc.at[gg, c], exc.at[gg, c], half_send.at[index], half_recv.at[index], partner
        )

    def half_arrival(gg, index):
        return remote(
            exc.at[gg, 1 - c], exc.at[gg, 1 - c], half_send.at[index], half_recv.at[index], partner
        )

    for o in range(4):
        share_here(o).wait()
    half_copy(g, 0).start()

    def cache_copy(d):
        peer = lax.rem(z + d, 4)
        return remote(pair.at[peer], cach.at[z], c_send.at[d], c_recv.at[d], at(g, peer * 2 + x, c))

    def cache_arrival(d):
        peer = lax.rem(z + 4 - d, 4)
        return remote(pair.at[0], cach.at[peer], c_send.at[d], c_recv.at[d], at(g, peer * 2 + x, c))

    swap_in.wait_recv()
    for d in range(1, 4):
        cache_copy(d).start()
    cach[z] = pair[z]

    for o in range(4):
        for k, xx in ((0, x), (4, 1 - x)):
            block = exc.at[1 - g, c, :, o, xx]
            remote(block, block, sy_send.at[k + o], sy_recv.at[k + o], across).wait_recv()
    half_copy(1 - g, 1).start()
    pump(3)
    half_arrival(g, 0).wait_recv()
    half_arrival(1 - g, 1).wait_recv()

    routes = {1: (g, 1 - x, side), 2: (1 - g, x, across), 3: (1 - g, 1 - x, corner)}

    def out_block(i, lanes, quarter):
        if i < 2:
            return spin.at[4 * i + quarter]
        return tin.at[4 * i - 8 + quarter, :, lanes]

    def out_copy(r, k):
        i, lanes = parts[k]
        gg, xx, dev = routes[r]
        src = outbox.at[r - 1, i] if i < 2 else outbox.at[r - 1, i, :, lanes]
        return remote(src, out_block(i, lanes, mine), out_send.at[r, k], out_recv.at[r, k], dev)

    def out_arrival(r, k):
        i, lanes = parts[k]
        gg, xx, dev = routes[r]
        block = out_block(i, lanes, 2 * gg + xx)
        return remote(block, block, out_send.at[r, k], out_recv.at[r, k], dev)

    whole = slice(0, 256)
    parts = [(0, whole), (1, whole), (2, halves[0]), (2, halves[1]), (3, halves[0]), (3, halves[1])]

    def spread_of(gg, xx, k):
        i, lanes = parts[k]
        if lanes == whole:
            low = jnp.concatenate([wbuf[i, 0, :512], wbuf[i, 1, :512]], axis=1)
            high = jnp.concatenate([wbuf[i, 0, 512:], wbuf[i, 1, 512:]], axis=1)
        else:
            h = lanes.start // 128
            low, high = wbuf[i, h, :512], wbuf[i, h, 512:]
        value = jnp.dot(exc[gg, 0, xx].reshape(256, 512), low, preferred_element_type=f32)
        value += jnp.dot(exc[gg, 1, xx].reshape(256, 512), high, preferred_element_type=f32)
        return value.astype(bf16)

    def produce(k):
        i, lanes = parts[k]
        for r in (3, 1, 2):
            gg, xx, dev = routes[r]
            outbox[r - 1, i, :, lanes] = spread_of(gg, xx, k)
            out_copy(r, k).start()
        value = spread_of(g, x, k)
        if i < 2:
            spin[4 * i + mine] = value
        else:
            tin[4 * i - 8 + mine, :, lanes] = value

    def placed(row):
        lanes = lax.broadcasted_iota(jnp.int32, (256, 128), 1)
        chosen = jnp.where(lax.rem(lanes, 16) == row, match[...], 0.0).astype(bf16)
        return jnp.dot(chosen, cach[...].reshape(128, 256), preferred_element_type=f32)

    def win_rows(i):
        return pl.ds(0, 6) if i == 0 else pl.ds(6, 4)

    def win_copy(i):
        block = win.at[c, win_rows(i)]
        return remote(block, block, win_send.at[i], win_recv.at[i], partner)

    def win_arrival(i):
        block = win.at[1 - c, win_rows(i)]
        return remote(block, block, win_send.at[i], win_recv.at[i], partner)

    def upsample(i):
        for r in (1, 2, 3):
            out_arrival(r, i).wait_recv()

        @pl.loop(4 * i, 4 * i + 4)
        def _(t):
            value = spin[t].astype(f32) + placed(t) + convb[...]
            ups[t] = value
            win[c, t + 2] = elu32(value).astype(bf16)

        win_copy(i).start()

    def decode(i):
        win_arrival(i).wait_recv()

        @pl.loop(0, 2)
        def _(p):
            t = 4 * i + 2 * p
            branch = jnp.zeros((512, 256), f32) + resb[...]
            for k in range(3):
                for h in range(2):
                    branch = branch + jnp.dot(
                        win[h, pl.ds(t + k, 2)].reshape(512, 256), resbuf[h, k],
                        preferred_element_type=f32,
                    )
            hidden = elu32(branch).astype(bf16)
            value = ups[pl.ds(t, 2)].reshape(512, 256) + jnp.dot(
                hidden, skipw[...], preferred_element_type=f32
            ) + skipb[...]
            for h in range(2):
                rows_dec[h, pl.ds(t, 256, stride=8), :] = value[:256, halves[h]]
                rows_dec[h, pl.ds(t + 1, 256, stride=8), :] = value[256:, halves[h]]

    produce(0)
    pump(4)
    res_in.wait_recv()
    for d in range(1, 4):
        cache_arrival(d).wait_recv()
    named = jnp.broadcast_to(cach[...].reshape(8, 16, 256).astype(f32)[:, 10:11, :], (8, 16, 256)).reshape(128, 256)
    sessions = lax.broadcasted_iota(jnp.int32, (128, 256), 1).astype(f32)
    match[...] = jnp.where(named == sessions, 1.0, 0.0).T
    for i in range(2):
        win[c, i] = placed(8 + i).astype(bf16)
    pump(5)
    produce(1)
    pump(6)
    produce(2)
    pump(7)
    produce(3)
    pump(8)
    produce(4)
    upsample(0)
    pump(9)
    produce(5)
    upsample(1)
    decode(0)
    decode(1)
    for h in range(2):
        dec_ref[:, :, halves[h]] = rows_dec[h].reshape(256, 8, 128).astype(bf16)

    def collect(k):
        i, lanes = parts[k]
        h = lanes.start // 128
        for r in (1, 2, 3):
            out_arrival(r, k).wait_recv()
        for t in range(4 * i - 8, 4 * i - 4):
            rows_tail[h, pl.ds(t, 256, stride=8), :] = tin[t, :, lanes].astype(f32)
        if i == 3:
            tail_ref[:, :, lanes] = rows_tail[h].reshape(256, 8, 128).astype(bf16)

    for k in range(2, 6):
        collect(k)

    for k in range(6):
        for r in (1, 2, 3):
            out_copy(r, k).wait_send()
    for i in range(2):
        win_copy(i).wait_send()
        half_copy((g, 1 - g)[i], i).wait_send()
    res_out.wait_send()
    swap_out.wait_send()
    for d in range(1, 4):
        cache_copy(d).wait_send()
    for o in range(4):
        share_side(o).wait_send()
        share_across(o).wait_send()
        relay_copy(o).wait_send()
    for hops in (1, 2, 3):
        pl.when(z + hops <= 3)(lambda: l_copy(hops, True).wait_send())
        pl.when(z - hops >= 0)(lambda: l_copy(hops, False).wait_send())

    for n in range(UNITS):
        cross(n).wait_send()
        for up, has in ((True, has_up), (False, has_down)):

            @pl.when(has)
            def _():
                plain(n, up).wait_send()
                crossed(n, up).wait_send()
                for s in (1, 2):
                    pl.when((z - s >= 0) if up else (z + s <= 3))(
                        lambda s=s: passed(n, s, up).wait_send()
                    )


def publish(dec_ref, tail_ref, dec_out, tail_out, sem):
    copies = (
        pltpu.make_async_copy(dec_ref, dec_out, sem.at[0]),
        pltpu.make_async_copy(tail_ref, tail_out, sem.at[1]),
    )
    for copy in copies:
        copy.start()
    for copy in copies:
        copy.wait()


def fused(
    latent, conv_weight, conv_bias, tail_cache, input_cache, resume_slot,
    res_weight, res_bias, skip_weight, skip_bias,
):
    dma = pltpu.SemaphoreType.DMA
    bf16, f32 = jnp.bfloat16, jnp.float32
    vmem = pl.BlockSpec(memory_space=pltpu.VMEM)
    anywhere = pl.BlockSpec(memory_space=pl.ANY)
    operands = [
        pltpu.with_memory_space_constraint(array, pltpu.HBM)
        for array in (
            latent, conv_weight, tail_cache, input_cache, resume_slot, conv_bias[None, :], res_weight,
            res_bias[None, :], skip_weight, skip_bias[None, :],
        )
    ]
    decoded, new_tail = pl.pallas_call(
        fused_kernel,
        out_shape=(
            jax.ShapeDtypeStruct((256, 8, 256), bf16),
            jax.ShapeDtypeStruct((256, 8, 256), bf16),
        ),
        in_specs=[anywhere] * 10,
        out_specs=(vmem,) * 2,
        scratch_shapes=[
            pltpu.VMEM((256, 512), bf16),
            pltpu.VMEM((128, 16, 256), bf16),
            pltpu.VMEM((2, 2048, 128), f32),
            pltpu.VMEM((8, 128, 128), bf16),
            pltpu.VMEM((8, 8, 256), bf16),
            pltpu.VMEM((8, 2, 256), bf16),
            pltpu.VMEM((256, 256), bf16),
            pltpu.VMEM((4, 2, 1024, 128), bf16),
            pltpu.VMEM((4, 4, 2, 32, 512), bf16),
            pltpu.VMEM((2, 2, 2, 4, 2, 32, 512), bf16),
            pltpu.VMEM((2, 4, 16, 256), bf16),
            pltpu.VMEM((4, 2, 16, 256), bf16),
            pltpu.VMEM((4, 2, 16, 256), bf16),
            pltpu.VMEM((8, 256, 256), bf16),
            pltpu.VMEM((8, 256, 256), bf16),
            pltpu.VMEM((3, 4, 256, 256), bf16),
            pltpu.VMEM((8, 256, 256), f32),
            pltpu.VMEM((2, 10, 256, 256), bf16),
            pltpu.VMEM((2, 3, 256, 256), bf16),
            pltpu.VMEM((256, 128), f32),
            pltpu.VMEM((2, 2048, 128), f32),
            pltpu.VMEM((2, 2048, 128), f32),
            pltpu.SMEM((8,), jnp.int32),
            pltpu.VMEM((1, 256), f32),
            pltpu.VMEM((1, 256), f32),
            pltpu.VMEM((1, 256), f32),
            dma((8, 2, 4)), dma((8, 2, 3)),
            dma((8,)), dma((8,)),
            dma((4,)), dma((4,)),
            dma((4,)), dma((4,)),
            dma((8,)), dma((8,)),
            dma((3,)), dma((3,)),
            dma((8,)), dma((8,)),
            dma((2,)), dma((2,)),
            dma((4, 6)), dma((4, 6)),
            dma((4,)), dma((10,)), pltpu.SemaphoreType.REGULAR((4,)),
        ],
        compiler_params=pltpu.CompilerParams(
            collective_id=0, has_side_effects=True, vmem_limit_bytes=48 * 1024 * 1024
        ),
    )(*operands)
    return pl.pallas_call(
        publish,
        out_shape=(
            jax.ShapeDtypeStruct((256, 8, 256), bf16),
            jax.ShapeDtypeStruct((256, 8, 256), bf16),
        ),
        in_specs=[vmem] * 2,
        out_specs=(anywhere,) * 2,
        scratch_shapes=[dma((2,))],
    )(*[pltpu.with_memory_space_constraint(array, pltpu.VMEM) for array in (decoded, new_tail)])


def solution(mesh):
    sizes = tuple(mesh.shape[name] for name in ("groups", "streams", "segment"))
    body = fused if sizes == (2, 8, 2) else local
    placed = (
        P(("groups", "streams"), "segment"),
        P("streams", None, "segment"),
        P("segment"),
        P(("groups", "streams"), None, "segment"),
        P(("groups", "streams"), None, "segment"),
        P(("groups", "streams")),
        P(None, "segment", None),
        P(),
        P(None, "segment"),
        P("segment"),
    )
    return jax.shard_map(
        body,
        mesh=mesh,
        in_specs=placed,
        out_specs=(
            P(("groups", "streams"), None, "segment"),
            P(("groups", "streams"), None, "segment"),
        ),
        check_vma=False,
    )
```

```python
import jax
import jax.numpy as jnp
from jax import lax
from jax.experimental import pallas as pl
from jax.experimental.pallas import tpu as pltpu
from jax.sharding import PartitionSpec as P


def apply_elu(values):
    return jnp.where(values > 0, values, jnp.expm1(jnp.minimum(values, 0.0)))


def local(
    latent,
    conv_weight,
    conv_bias,
    tail_cache,
    input_cache,
    resume_slot,
    res_weight,
    res_bias,
    skip_weight,
    skip_bias,
):
    handed = lax.all_to_all(latent, "streams", split_axis=0, concat_axis=0, tiled=True)
    excitation_half = apply_elu(handed.astype(jnp.float32)).astype(jnp.bfloat16)
    excitation = lax.all_gather(excitation_half, "segment", axis=1, tiled=True)
    session_rows = excitation.shape[0]
    tap_count = conv_weight.shape[1]
    half_taps = tap_count // 2
    half_width = conv_weight.shape[2]
    piece = lax.all_gather(conv_weight, "streams", axis=0, tiled=True)
    kernel_rows = piece.reshape(piece.shape[0], tap_count * half_width)
    spread = jnp.dot(excitation, kernel_rows, preferred_element_type=jnp.float32)
    spread = spread.reshape(session_rows, tap_count, half_width)
    fetched_tail, fetched_input, fetched_slot = (
        lax.all_to_all(tail_cache, "streams", split_axis=0, concat_axis=0, tiled=True),
        lax.all_to_all(input_cache, "streams", split_axis=0, concat_axis=0, tiled=True),
        lax.all_to_all(resume_slot, "streams", split_axis=0, concat_axis=0, tiled=True),
    )
    arrivals = fetched_slot.shape[0]
    state_steps = fetched_input.shape[1]
    packed = jnp.concatenate(
        [fetched_tail.reshape(arrivals, -1), fetched_input.reshape(arrivals, -1)], axis=1
    )
    one_hot = (fetched_slot[None, :] == jnp.arange(session_rows, dtype=jnp.int32)[:, None]).astype(
        jnp.bfloat16
    )
    placed = jnp.dot(one_hot, packed, preferred_element_type=jnp.float32)
    prev_tail = placed[:, : half_taps * half_width].reshape(session_rows, half_taps, half_width)
    prev_input = (
        placed[:, half_taps * half_width :]
        .reshape(session_rows, state_steps, half_width)
        .astype(jnp.bfloat16)
    )
    upsampled = spread[:, :half_taps] + prev_tail + conv_bias
    new_tail = spread[:, half_taps:].astype(jnp.bfloat16)
    excited = apply_elu(upsampled).astype(jnp.bfloat16)
    window = jnp.concatenate([prev_input, excited], axis=1)
    hidden_width = res_weight.shape[2]
    partial_value = jnp.zeros((session_rows * half_taps, hidden_width), jnp.float32)
    for offset in range(res_weight.shape[0]):
        frames = window[:, offset : offset + half_taps].reshape(
            session_rows * half_taps, half_width
        )
        partial_value = partial_value + jnp.dot(
            frames, res_weight[offset], preferred_element_type=jnp.float32
        )
    partial_value = partial_value.reshape(session_rows, half_taps, hidden_width)
    summed = lax.psum(partial_value, "segment")
    hidden = apply_elu(summed + res_bias).astype(jnp.bfloat16)
    projected = jnp.dot(
        hidden.reshape(session_rows * half_taps, hidden_width),
        skip_weight,
        preferred_element_type=jnp.float32,
    )
    decoded_block = upsampled + projected.reshape(session_rows, half_taps, half_width) + skip_bias
    return (decoded_block.astype(jnp.bfloat16), new_tail)


UNITS = 8
AHEAD = 2
MESH = pl.DeviceIdType.MESH


def elu32(values):
    return jnp.where(values > 0, values, jnp.exp(jnp.minimum(values, 0.0)) - 1.0)


def fused_kernel(
    lat_hbm, w_hbm, tailc_hbm, inpc_hbm, slot_hbm, convb_hbm, resw_hbm, resb_hbm, skipw_hbm, skipb_hbm,
    dec_ref, tail_ref,
    latv, wraw, wide, wside, tailc, inpc, skipw, wbuf, lst, exc, pack, pair, cach, spin, tin, outbox, ups, win, resbuf, match, rows_dec, rows_tail,
    slots, convb, resb, skipb,
    w_send, w_recv, x_send, x_recv, l_send, l_recv, sx_send, sx_recv, sy_send, sy_recv,
    half_send, half_recv, c_send, c_recv, win_send, win_recv, out_send, out_recv, sl_sem, local_sem,
):
    g = lax.axis_index("groups")
    j = lax.axis_index("streams")
    c = lax.axis_index("segment")
    z, x = j // 2, lax.rem(j, 2)
    jx = z * 2 + 1 - x
    mine = 2 * g + x
    theirs = 2 * g + 1 - x
    f32, bf16 = jnp.float32, jnp.bfloat16

    def at(gg, jj, cc):
        return {"groups": gg, "streams": jj, "segment": cc}

    def remote(src, dst, ss, rs, dev):
        return pltpu.make_async_remote_copy(
            src_ref=src, dst_ref=dst, send_sem=ss, recv_sem=rs, device_id=dev, device_id_type=MESH
        )

    partner = at(g, j, 1 - c)
    side = at(g, jx, c)
    across = at(1 - g, j, c)
    corner = at(1 - g, jx, c)
    above = at(g, j + 2, c)
    below = at(g, j - 2, c)
    has_up, has_down = z < 3, z > 0

    barrier = pltpu.get_barrier_semaphore()

    def greet(dev):
        pl.semaphore_signal(barrier, inc=1, device_id=dev, device_id_type=MESH)

    greet(side)
    greet(across)
    greet(partner)
    pl.when(has_up)(lambda: greet(above))
    pl.when(has_down)(lambda: greet(below))

    halves = (slice(0, 128), slice(128, 256))
    own_lat = pltpu.make_async_copy(lat_hbm, latv, local_sem.at[4])
    own_w = pltpu.make_async_copy(w_hbm, wraw, local_sem.at[5])
    own_res = pltpu.make_async_copy(resw_hbm, resbuf.at[c], local_sem.at[1])
    small = [
        pltpu.make_async_copy(tailc_hbm, tailc, local_sem.at[7]),
        pltpu.make_async_copy(inpc_hbm, inpc, local_sem.at[8]),
        pltpu.make_async_copy(skipw_hbm, skipw, local_sem.at[9]),
        pltpu.make_async_copy(slot_hbm, slots, local_sem.at[0]),
        pltpu.make_async_copy(convb_hbm, convb, local_sem.at[2]),
        pltpu.make_async_copy(resb_hbm, resb, local_sem.at[3]),
        pltpu.make_async_copy(skipb_hbm, skipb, local_sem.at[6]),
    ]
    own_lat.start()
    own_w.start()
    own_res.start()
    for copy in small:
        copy.start()

    def regroup(i):
        for quarter in (theirs, mine):
            for h in range(2):
                block = wide[h, pl.ds(4 * i + quarter, 128, stride=16), :].astype(bf16)
                if quarter is theirs:
                    wside[2 * i + h] = block
                else:
                    wbuf[i, h, pl.ds(j * 128, 128)] = block

    own_lat.wait()
    lst[z] = elu32(latv[...].astype(f32)).astype(bf16).reshape(4, 2, 32, 512)

    pl.semaphore_wait(barrier, 3 + jnp.where(has_up, 1, 0) + jnp.where(has_down, 1, 0))

    def l_copy(s, d, up):
        block = lst.at[z - s if up else z + s, d]
        k = 0 if up else 1
        return remote(block, block, l_send.at[k, s, d], l_recv.at[k, s, d], above if up else below)

    def l_arrival(s, d, up):
        block = lst.at[z - 1 - s if up else z + 1 + s, d]
        k = 0 if up else 1
        return remote(block, block, l_send.at[k, s, d], l_recv.at[k, s, d], below if up else above)

    def share_side(o):
        return remote(lst.at[o, z], exc.at[g, c, :, o, x], sx_send.at[o], sx_recv.at[o], side)

    def share_across(o):
        return remote(lst.at[o, z], exc.at[g, c, :, o, x], sy_send.at[o], sy_recv.at[o], across)

    def share_here(o):
        return pltpu.make_async_copy(lst.at[o, z], exc.at[g, c, :, o, x], sl_sem.at[o])

    def share(o):
        share_side(o).start()
        share_across(o).start()
        share_here(o).start()

    def relay_copy(o):
        block = exc.at[g, c, :, o, 1 - x]
        return remote(block, block, sy_send.at[4 + o], sy_recv.at[4 + o], across)

    def relay(o):
        block = exc.at[g, c, :, o, 1 - x]
        remote(block, block, sx_send.at[o], sx_recv.at[o], side).wait_recv()
        relay_copy(o).start()

    def l_step(s):
        @pl.when(z - 1 - s >= 0)
        def _():
            for d in range(3, s, -1):

                @pl.when(d >= z)
                def _():
                    l_arrival(s, d, True).wait_recv()

                if d >= s + 2:

                    @pl.when(d > z)
                    def _():
                        l_copy(s + 1, d, True).start()

            share(z - 1 - s)

        @pl.when(z + 1 + s <= 3)
        def _():
            for d in range(0, 3 - s):

                @pl.when(d <= z)
                def _():
                    l_arrival(s, d, False).wait_recv()

                if d <= 1 - s:

                    @pl.when(d < z)
                    def _():
                        l_copy(s + 1, d, False).start()

            share(z + 1 + s)

    def relay_step(s):
        pl.when(z - 1 - s >= 0)(lambda: relay(z - 1 - s))
        pl.when(z + 1 + s <= 3)(lambda: relay(z + 1 + s))

    def cross(n):
        return remote(
            wside.at[n], wbuf.at[n // 2, n % 2, pl.ds(j * 128, 128)], x_send.at[n], x_recv.at[n], side
        )

    def plain(n, up):
        k = 0 if up else 1
        block = wbuf.at[n // 2, n % 2, pl.ds(j * 128, 128)]
        return remote(
            block, block, w_send.at[n, k, 0], w_recv.at[n, k, 0], above if up else below
        )

    def crossed(n, up):
        k = 0 if up else 1
        block = wbuf.at[n // 2, n % 2, pl.ds(jx * 128, 128)]
        return remote(block, block, w_send.at[n, k, 1], w_recv.at[n, k, 0], above if up else below)

    def passed(n, s, up):
        k = 0 if up else 1
        block = wbuf.at[n // 2, n % 2, pl.ds((z - s if up else z + s) * 256, 256)]
        return remote(block, block, w_send.at[n, k, 1 + s], w_recv.at[n, k, s], above if up else below)

    def arrival(n, s, up):
        k = 0 if up else 1
        block = wbuf.at[n // 2, n % 2, pl.ds((z - 1 - s if up else z + 1 + s) * 256, 256)]
        return remote(block, block, w_send.at[n, k, 1 + s], w_recv.at[n, k, s], below if up else above)

    def send_plain(n):
        pl.when(has_up)(lambda: plain(n, True).start())
        pl.when(has_down)(lambda: plain(n, False).start())

    def send_crossed(n):
        block = wbuf.at[n // 2, n % 2, pl.ds(jx * 128, 128)]
        remote(block, block, x_send.at[n], x_recv.at[n], side).wait_recv()
        pl.when(has_up)(lambda: crossed(n, True).start())
        pl.when(has_down)(lambda: crossed(n, False).start())

    def forward(n, s):
        @pl.when(z - 1 - s >= 0)
        def _():
            arrival(n, s, True).wait_recv()
            if s < 2:
                pl.when(has_up)(lambda: passed(n, s + 1, True).start())

        @pl.when(z + 1 + s <= 3)
        def _():
            arrival(n, s, False).wait_recv()
            if s < 2:
                pl.when(has_down)(lambda: passed(n, s + 1, False).start())

    def pump(tick):
        for s in (1, 0):
            if 0 <= tick - s < UNITS:
                forward(tick - s, s)
        n = tick + AHEAD
        if n < UNITS:
            send_plain(n)
            send_crossed(n)
        if n + 2 < UNITS:
            cross(n + 2).start()
        if 0 <= tick - 2 < UNITS:
            forward(tick - 2, 2)

    for d in (3, 2, 1):
        pl.when(d > z)(lambda d=d: l_copy(0, d, True).start())
    for d in (0, 1, 2):
        pl.when(d < z)(lambda d=d: l_copy(0, d, False).start())
    share(z)
    own_w.wait()
    for h in range(2):
        wide[h] = wraw[:, :, halves[h]].reshape(2048, 128).astype(f32)
    regroup(0)
    cross(0).start()
    cross(1).start()
    send_plain(0)
    for i in range(1, 4):
        regroup(i)
    for n in range(2, AHEAD + 2):
        cross(n).start()
    own_res.wait()
    res_out = remote(resbuf.at[c], resbuf.at[c], half_send.at[2], half_recv.at[2], partner)
    res_in = remote(resbuf.at[c], resbuf.at[1 - c], half_send.at[2], half_recv.at[2], partner)
    res_out.start()

    for copy in small:
        copy.wait()
    for d in range(8):
        pack[d % 2, d // 2] = jnp.concatenate(
            [
                tailc[d].astype(f32),
                inpc[d].astype(f32),
                jnp.full((6, 256), slots[d].astype(f32)),
            ],
            axis=0,
        ).astype(bf16)

    swap_out = remote(pack.at[1 - x], pair.at[:, x], c_send.at[0], c_recv.at[0], side)
    swap_in = remote(pack.at[1 - x], pair.at[:, 1 - x], c_send.at[0], c_recv.at[0], side)
    swap_out.start()
    pair[:, x] = pack[x]

    send_crossed(0)
    send_plain(1)
    send_crossed(1)
    l_step(0)
    relay(z)
    for n in range(2, AHEAD):
        send_plain(n)
        send_crossed(n)
    pump(0)
    l_step(1)
    relay_step(0)
    pump(1)
    l_step(2)
    relay_step(1)
    pump(2)
    relay_step(2)

    def half_copy(gg, index):
        return remote(
            exc.at[gg, c], exc.at[gg, c], half_send.at[index], half_recv.at[index], partner
        )

    def half_arrival(gg, index):
        return remote(
            exc.at[gg, 1 - c], exc.at[gg, 1 - c], half_send.at[index], half_recv.at[index], partner
        )

    for o in range(4):
        share_here(o).wait()
    half_copy(g, 0).start()

    def cache_copy(d):
        peer = lax.rem(z + d, 4)
        return remote(pair.at[peer], cach.at[z], c_send.at[d], c_recv.at[d], at(g, peer * 2 + x, c))

    def cache_arrival(d):
        peer = lax.rem(z + 4 - d, 4)
        return remote(pair.at[0], cach.at[peer], c_send.at[d], c_recv.at[d], at(g, peer * 2 + x, c))

    swap_in.wait_recv()
    for d in range(1, 4):
        cache_copy(d).start()
    cach[z] = pair[z]

    for o in range(4):
        for k, xx in ((0, x), (4, 1 - x)):
            block = exc.at[1 - g, c, :, o, xx]
            remote(block, block, sy_send.at[k + o], sy_recv.at[k + o], across).wait_recv()
    half_copy(1 - g, 1).start()
    pump(3)
    half_arrival(g, 0).wait_recv()
    half_arrival(1 - g, 1).wait_recv()

    routes = {1: (g, 1 - x, side), 2: (1 - g, x, across), 3: (1 - g, 1 - x, corner)}

    def out_block(i, lanes, quarter):
        if i < 2:
            return spin.at[4 * i + quarter]
        return tin.at[4 * i - 8 + quarter, :, lanes]

    def out_copy(r, k):
        i, lanes = parts[k]
        gg, xx, dev = routes[r]
        src = outbox.at[r - 1, i] if i < 2 else outbox.at[r - 1, i, :, lanes]
        return remote(src, out_block(i, lanes, mine), out_send.at[r, k], out_recv.at[r, k], dev)

    def out_arrival(r, k):
        i, lanes = parts[k]
        gg, xx, dev = routes[r]
        block = out_block(i, lanes, 2 * gg + xx)
        return remote(block, block, out_send.at[r, k], out_recv.at[r, k], dev)

    whole = slice(0, 256)
    parts = [(0, whole), (1, whole), (2, halves[0]), (2, halves[1]), (3, halves[0]), (3, halves[1])]

    def spread_of(gg, xx, k):
        i, lanes = parts[k]
        if lanes == whole:
            low = jnp.concatenate([wbuf[i, 0, :512], wbuf[i, 1, :512]], axis=1)
            high = jnp.concatenate([wbuf[i, 0, 512:], wbuf[i, 1, 512:]], axis=1)
        else:
            h = lanes.start // 128
            low, high = wbuf[i, h, :512], wbuf[i, h, 512:]
        value = jnp.dot(exc[gg, 0, xx].reshape(256, 512), low, preferred_element_type=f32)
        value += jnp.dot(exc[gg, 1, xx].reshape(256, 512), high, preferred_element_type=f32)
        return value.astype(bf16)

    def produce(k):
        i, lanes = parts[k]
        for r in (3, 1, 2):
            gg, xx, dev = routes[r]
            outbox[r - 1, i, :, lanes] = spread_of(gg, xx, k)
            out_copy(r, k).start()
        value = spread_of(g, x, k)
        if i < 2:
            spin[4 * i + mine] = value
        else:
            tin[4 * i - 8 + mine, :, lanes] = value

    def placed(row):
        lanes = lax.broadcasted_iota(jnp.int32, (256, 128), 1)
        chosen = jnp.where(lax.rem(lanes, 16) == row, match[...], 0.0).astype(bf16)
        return jnp.dot(chosen, cach[...].reshape(128, 256), preferred_element_type=f32)

    def win_rows(i):
        return pl.ds(0, 6) if i == 0 else pl.ds(6, 4)

    def win_copy(i):
        block = win.at[c, win_rows(i)]
        return remote(block, block, win_send.at[i], win_recv.at[i], partner)

    def win_arrival(i):
        block = win.at[1 - c, win_rows(i)]
        return remote(block, block, win_send.at[i], win_recv.at[i], partner)

    def upsample(i):
        for r in (1, 2, 3):
            out_arrival(r, i).wait_recv()

        @pl.loop(4 * i, 4 * i + 4)
        def _(t):
            value = spin[t].astype(f32) + placed(t) + convb[...]
            ups[t] = value
            win[c, t + 2] = elu32(value).astype(bf16)

        win_copy(i).start()

    def decode(i):
        win_arrival(i).wait_recv()

        @pl.loop(0, 2)
        def _(p):
            t = 4 * i + 2 * p
            branch = jnp.zeros((512, 256), f32) + resb[...]
            for k in range(3):
                for h in range(2):
                    branch = branch + jnp.dot(
                        win[h, pl.ds(t + k, 2)].reshape(512, 256), resbuf[h, k],
                        preferred_element_type=f32,
                    )
            hidden = elu32(branch).astype(bf16)
            value = ups[pl.ds(t, 2)].reshape(512, 256) + jnp.dot(
                hidden, skipw[...], preferred_element_type=f32
            ) + skipb[...]
            for h in range(2):
                rows_dec[h, pl.ds(t, 256, stride=8), :] = value[:256, halves[h]]
                rows_dec[h, pl.ds(t + 1, 256, stride=8), :] = value[256:, halves[h]]

    produce(0)
    pump(4)
    res_in.wait_recv()
    for d in range(1, 4):
        cache_arrival(d).wait_recv()
    named = jnp.broadcast_to(cach[...].reshape(8, 16, 256).astype(f32)[:, 10:11, :], (8, 16, 256)).reshape(128, 256)
    sessions = lax.broadcasted_iota(jnp.int32, (128, 256), 1).astype(f32)
    match[...] = jnp.where(named == sessions, 1.0, 0.0).T
    for i in range(2):
        win[c, i] = placed(8 + i).astype(bf16)
    pump(5)
    produce(1)
    pump(6)
    produce(2)
    pump(7)
    produce(3)
    pump(8)
    produce(4)
    upsample(0)
    pump(9)
    produce(5)
    upsample(1)
    decode(0)
    decode(1)
    for h in range(2):
        dec_ref[:, :, halves[h]] = rows_dec[h].reshape(256, 8, 128).astype(bf16)

    def collect(k):
        i, lanes = parts[k]
        h = lanes.start // 128
        for r in (1, 2, 3):
            out_arrival(r, k).wait_recv()
        for t in range(4 * i - 8, 4 * i - 4):
            rows_tail[h, pl.ds(t, 256, stride=8), :] = tin[t, :, lanes].astype(f32)
        if i == 3:
            tail_ref[:, :, lanes] = rows_tail[h].reshape(256, 8, 128).astype(bf16)

    for k in range(2, 6):
        collect(k)

    for k in range(6):
        for r in (1, 2, 3):
            out_copy(r, k).wait_send()
    for i in range(2):
        win_copy(i).wait_send()
        half_copy((g, 1 - g)[i], i).wait_send()
    res_out.wait_send()
    swap_out.wait_send()
    for d in range(1, 4):
        cache_copy(d).wait_send()
    for o in range(4):
        share_side(o).wait_send()
        share_across(o).wait_send()
        relay_copy(o).wait_send()
    for s in range(3):
        for d in range(4):
            if d >= s + 1:
                pl.when((z - s >= 0) & (d > z))(lambda s=s, d=d: l_copy(s, d, True).wait_send())
            if d <= 2 - s:
                pl.when((z + s <= 3) & (d < z))(lambda s=s, d=d: l_copy(s, d, False).wait_send())

    for n in range(UNITS):
        cross(n).wait_send()
        for up, has in ((True, has_up), (False, has_down)):

            @pl.when(has)
            def _():
                plain(n, up).wait_send()
                crossed(n, up).wait_send()
                for s in (1, 2):
                    pl.when((z - s >= 0) if up else (z + s <= 3))(
                        lambda s=s: passed(n, s, up).wait_send()
                    )


def publish(dec_ref, tail_ref, dec_out, tail_out, sem):
    copies = (
        pltpu.make_async_copy(dec_ref, dec_out, sem.at[0]),
        pltpu.make_async_copy(tail_ref, tail_out, sem.at[1]),
    )
    for copy in copies:
        copy.start()
    for copy in copies:
        copy.wait()


def fused(
    latent, conv_weight, conv_bias, tail_cache, input_cache, resume_slot,
    res_weight, res_bias, skip_weight, skip_bias,
):
    dma = pltpu.SemaphoreType.DMA
    bf16, f32 = jnp.bfloat16, jnp.float32
    vmem = pl.BlockSpec(memory_space=pltpu.VMEM)
    anywhere = pl.BlockSpec(memory_space=pl.ANY)
    operands = [
        pltpu.with_memory_space_constraint(array, pltpu.HBM)
        for array in (
            latent, conv_weight, tail_cache, input_cache, resume_slot, conv_bias[None, :], res_weight,
            res_bias[None, :], skip_weight, skip_bias[None, :],
        )
    ]
    decoded, new_tail = pl.pallas_call(
        fused_kernel,
        out_shape=(
            jax.ShapeDtypeStruct((256, 8, 256), bf16),
            jax.ShapeDtypeStruct((256, 8, 256), bf16),
        ),
        in_specs=[anywhere] * 10,
        out_specs=(vmem,) * 2,
        scratch_shapes=[
            pltpu.VMEM((256, 512), bf16),
            pltpu.VMEM((128, 16, 256), bf16),
            pltpu.VMEM((2, 2048, 128), f32),
            pltpu.VMEM((8, 128, 128), bf16),
            pltpu.VMEM((8, 8, 256), bf16),
            pltpu.VMEM((8, 2, 256), bf16),
            pltpu.VMEM((256, 256), bf16),
            pltpu.VMEM((4, 2, 1024, 128), bf16),
            pltpu.VMEM((4, 4, 2, 32, 512), bf16),
            pltpu.VMEM((2, 2, 2, 4, 2, 32, 512), bf16),
            pltpu.VMEM((2, 4, 16, 256), bf16),
            pltpu.VMEM((4, 2, 16, 256), bf16),
            pltpu.VMEM((4, 2, 16, 256), bf16),
            pltpu.VMEM((8, 256, 256), bf16),
            pltpu.VMEM((8, 256, 256), bf16),
            pltpu.VMEM((3, 4, 256, 256), bf16),
            pltpu.VMEM((8, 256, 256), f32),
            pltpu.VMEM((2, 10, 256, 256), bf16),
            pltpu.VMEM((2, 3, 256, 256), bf16),
            pltpu.VMEM((256, 128), f32),
            pltpu.VMEM((2, 2048, 128), f32),
            pltpu.VMEM((2, 2048, 128), f32),
            pltpu.SMEM((8,), jnp.int32),
            pltpu.VMEM((1, 256), f32),
            pltpu.VMEM((1, 256), f32),
            pltpu.VMEM((1, 256), f32),
            dma((8, 2, 4)), dma((8, 2, 3)),
            dma((8,)), dma((8,)),
            dma((2, 3, 4)), dma((2, 3, 4)),
            dma((4,)), dma((4,)),
            dma((8,)), dma((8,)),
            dma((3,)), dma((3,)),
            dma((8,)), dma((8,)),
            dma((2,)), dma((2,)),
            dma((4, 6)), dma((4, 6)),
            dma((4,)), dma((10,)),
        ],
        compiler_params=pltpu.CompilerParams(
            collective_id=0, has_side_effects=True, vmem_limit_bytes=48 * 1024 * 1024
        ),
    )(*operands)
    return pl.pallas_call(
        publish,
        out_shape=(
            jax.ShapeDtypeStruct((256, 8, 256), bf16),
            jax.ShapeDtypeStruct((256, 8, 256), bf16),
        ),
        in_specs=[vmem] * 2,
        out_specs=(anywhere,) * 2,
        scratch_shapes=[dma((2,))],
    )(*[pltpu.with_memory_space_constraint(array, pltpu.VMEM) for array in (decoded, new_tail)])


def solution(mesh):
    sizes = tuple(mesh.shape[name] for name in ("groups", "streams", "segment"))
    body = fused if sizes == (2, 8, 2) else local
    placed = (
        P(("groups", "streams"), "segment"),
        P("streams", None, "segment"),
        P("segment"),
        P(("groups", "streams"), None, "segment"),
        P(("groups", "streams"), None, "segment"),
        P(("groups", "streams")),
        P(None, "segment", None),
        P(),
        P(None, "segment"),
        P("segment"),
    )
    return jax.shard_map(
        body,
        mesh=mesh,
        in_specs=placed,
        out_specs=(
            P(("groups", "streams"), None, "segment"),
            P(("groups", "streams"), None, "segment"),
        ),
        check_vma=False,
    )
```

```python
import jax
import jax.numpy as jnp
from jax import lax
from jax.experimental import pallas as pl
from jax.experimental.pallas import tpu as pltpu
from jax.sharding import PartitionSpec as P


def apply_elu(values):
    return jnp.where(values > 0, values, jnp.expm1(jnp.minimum(values, 0.0)))


def local(
    latent,
    conv_weight,
    conv_bias,
    tail_cache,
    input_cache,
    resume_slot,
    res_weight,
    res_bias,
    skip_weight,
    skip_bias,
):
    handed = lax.all_to_all(latent, "streams", split_axis=0, concat_axis=0, tiled=True)
    excitation_half = apply_elu(handed.astype(jnp.float32)).astype(jnp.bfloat16)
    excitation = lax.all_gather(excitation_half, "segment", axis=1, tiled=True)
    session_rows = excitation.shape[0]
    tap_count = conv_weight.shape[1]
    half_taps = tap_count // 2
    half_width = conv_weight.shape[2]
    piece = lax.all_gather(conv_weight, "streams", axis=0, tiled=True)
    kernel_rows = piece.reshape(piece.shape[0], tap_count * half_width)
    spread = jnp.dot(excitation, kernel_rows, preferred_element_type=jnp.float32)
    spread = spread.reshape(session_rows, tap_count, half_width)
    fetched_tail, fetched_input, fetched_slot = (
        lax.all_to_all(tail_cache, "streams", split_axis=0, concat_axis=0, tiled=True),
        lax.all_to_all(input_cache, "streams", split_axis=0, concat_axis=0, tiled=True),
        lax.all_to_all(resume_slot, "streams", split_axis=0, concat_axis=0, tiled=True),
    )
    arrivals = fetched_slot.shape[0]
    state_steps = fetched_input.shape[1]
    packed = jnp.concatenate(
        [fetched_tail.reshape(arrivals, -1), fetched_input.reshape(arrivals, -1)], axis=1
    )
    one_hot = (fetched_slot[None, :] == jnp.arange(session_rows, dtype=jnp.int32)[:, None]).astype(
        jnp.bfloat16
    )
    placed = jnp.dot(one_hot, packed, preferred_element_type=jnp.float32)
    prev_tail = placed[:, : half_taps * half_width].reshape(session_rows, half_taps, half_width)
    prev_input = (
        placed[:, half_taps * half_width :]
        .reshape(session_rows, state_steps, half_width)
        .astype(jnp.bfloat16)
    )
    upsampled = spread[:, :half_taps] + prev_tail + conv_bias
    new_tail = spread[:, half_taps:].astype(jnp.bfloat16)
    excited = apply_elu(upsampled).astype(jnp.bfloat16)
    window = jnp.concatenate([prev_input, excited], axis=1)
    hidden_width = res_weight.shape[2]
    partial_value = jnp.zeros((session_rows * half_taps, hidden_width), jnp.float32)
    for offset in range(res_weight.shape[0]):
        frames = window[:, offset : offset + half_taps].reshape(
            session_rows * half_taps, half_width
        )
        partial_value = partial_value + jnp.dot(
            frames, res_weight[offset], preferred_element_type=jnp.float32
        )
    partial_value = partial_value.reshape(session_rows, half_taps, hidden_width)
    summed = lax.psum(partial_value, "segment")
    hidden = apply_elu(summed + res_bias).astype(jnp.bfloat16)
    projected = jnp.dot(
        hidden.reshape(session_rows * half_taps, hidden_width),
        skip_weight,
        preferred_element_type=jnp.float32,
    )
    decoded_block = upsampled + projected.reshape(session_rows, half_taps, half_width) + skip_bias
    return (decoded_block.astype(jnp.bfloat16), new_tail)


UNITS = 8
AHEAD = 2
MESH = pl.DeviceIdType.MESH


def elu32(values):
    return jnp.where(values > 0, values, jnp.exp(jnp.minimum(values, 0.0)) - 1.0)


def fused_kernel(
    lat_hbm, w_hbm, tailc_hbm, inpc_hbm, slot_hbm, convb_hbm, resw_hbm, resb_hbm, skipw_hbm, skipb_hbm,
    dec_ref, tail_ref,
    latv, wraw, wide, wside, tailc, inpc, skipw, wbuf, lst, exc, pack, pair, cach, spin, tin, outbox, ups, win, resbuf, match, rows_dec, rows_tail,
    slots, convb, resb, skipb,
    w_send, w_recv, x_send, x_recv, l_send, l_recv, sx_send, sx_recv, sy_send, sy_recv,
    half_send, half_recv, c_send, c_recv, win_send, win_recv, out_send, out_recv, sl_sem, local_sem, news,
):
    g = lax.axis_index("groups")
    j = lax.axis_index("streams")
    c = lax.axis_index("segment")
    z, x = j // 2, lax.rem(j, 2)
    jx = z * 2 + 1 - x
    mine = 2 * g + x
    theirs = 2 * g + 1 - x
    f32, bf16 = jnp.float32, jnp.bfloat16

    def at(gg, jj, cc):
        return {"groups": gg, "streams": jj, "segment": cc}

    def remote(src, dst, ss, rs, dev):
        return pltpu.make_async_remote_copy(
            src_ref=src, dst_ref=dst, send_sem=ss, recv_sem=rs, device_id=dev, device_id_type=MESH
        )

    partner = at(g, j, 1 - c)
    side = at(g, jx, c)
    across = at(1 - g, j, c)
    corner = at(1 - g, jx, c)
    above = at(g, j + 2, c)
    below = at(g, j - 2, c)
    has_up, has_down = z < 3, z > 0

    barrier = pltpu.get_barrier_semaphore()

    def greet(dev):
        pl.semaphore_signal(barrier, inc=1, device_id=dev, device_id_type=MESH)

    greet(side)
    greet(across)
    greet(partner)
    pl.when(has_up)(lambda: greet(above))
    pl.when(has_down)(lambda: greet(below))

    halves = (slice(0, 128), slice(128, 256))
    own_lat = pltpu.make_async_copy(lat_hbm, latv, local_sem.at[4])
    own_w = pltpu.make_async_copy(w_hbm, wraw, local_sem.at[5])
    own_res = pltpu.make_async_copy(resw_hbm, resbuf.at[c], local_sem.at[1])
    small = [
        pltpu.make_async_copy(tailc_hbm, tailc, local_sem.at[7]),
        pltpu.make_async_copy(inpc_hbm, inpc, local_sem.at[8]),
        pltpu.make_async_copy(skipw_hbm, skipw, local_sem.at[9]),
        pltpu.make_async_copy(slot_hbm, slots, local_sem.at[0]),
        pltpu.make_async_copy(convb_hbm, convb, local_sem.at[2]),
        pltpu.make_async_copy(resb_hbm, resb, local_sem.at[3]),
        pltpu.make_async_copy(skipb_hbm, skipb, local_sem.at[6]),
    ]
    own_lat.start()
    own_w.start()
    own_res.start()
    for copy in small:
        copy.start()

    def regroup(i):
        for quarter in (theirs, mine):
            for h in range(2):
                block = wide[h, pl.ds(4 * i + quarter, 128, stride=16), :].astype(bf16)
                if quarter is theirs:
                    wside[2 * i + h] = block
                else:
                    wbuf[i, h, pl.ds(j * 128, 128)] = block

    own_lat.wait()
    lst[z] = elu32(latv[...].astype(f32)).astype(bf16).reshape(4, 2, 32, 512)

    pl.semaphore_wait(barrier, 3 + jnp.where(has_up, 1, 0) + jnp.where(has_down, 1, 0))

    def line(zz):
        return at(g, zz * 2 + x, c)

    def l_copy(hops, up):
        d = z + hops if up else z - hops
        return remote(lst.at[z, d], lst.at[z, d], l_send.at[d], l_recv.at[z], line(d))

    def l_arrival(o):
        return remote(lst.at[o, z], lst.at[o, z], l_send.at[o], l_recv.at[o], line(o))

    def l_send_out(hops):
        pl.when(z + hops <= 3)(lambda: l_copy(hops, True).start())
        pl.when(z - hops >= 0)(lambda: l_copy(hops, False).start())

    def tell(index, dev):
        pl.semaphore_signal(news.at[index], inc=1, device_id=dev, device_id_type=MESH)

    def tell_second():
        @pl.when((z > 0) & (z < 3))
        def _():
            tell(0, below)
            tell(1, above)

    def hear_second():
        pl.when(z <= 1)(lambda: pl.semaphore_wait(news.at[0], 1))
        pl.when(z >= 2)(lambda: pl.semaphore_wait(news.at[1], 1))
        pl.when(z == 1)(lambda: tell(2, below))
        pl.when(z == 2)(lambda: tell(3, above))

    def hear_third():
        pl.when(z == 0)(lambda: pl.semaphore_wait(news.at[2], 1))
        pl.when(z == 3)(lambda: pl.semaphore_wait(news.at[3], 1))

    def share_side(o):
        return remote(lst.at[o, z], exc.at[g, c, :, o, x], sx_send.at[o], sx_recv.at[o], side)

    def share_across(o):
        return remote(lst.at[o, z], exc.at[g, c, :, o, x], sy_send.at[o], sy_recv.at[o], across)

    def share_here(o):
        return pltpu.make_async_copy(lst.at[o, z], exc.at[g, c, :, o, x], sl_sem.at[o])

    def share(o):
        share_side(o).start()
        share_across(o).start()
        share_here(o).start()

    def relay_copy(o):
        block = exc.at[g, c, :, o, 1 - x]
        return remote(block, block, sy_send.at[4 + o], sy_recv.at[4 + o], across)

    def relay(o):
        block = exc.at[g, c, :, o, 1 - x]
        remote(block, block, sx_send.at[o], sx_recv.at[o], side).wait_recv()
        relay_copy(o).start()

    def l_step(s):
        for o, there in ((z - 1 - s, z - 1 - s >= 0), (z + 1 + s, z + 1 + s <= 3)):

            @pl.when(there)
            def _():
                l_arrival(o).wait_recv()
                share(o)

    def relay_step(s):
        pl.when(z - 1 - s >= 0)(lambda: relay(z - 1 - s))
        pl.when(z + 1 + s <= 3)(lambda: relay(z + 1 + s))

    def cross(n):
        return remote(
            wside.at[n], wbuf.at[n // 2, n % 2, pl.ds(j * 128, 128)], x_send.at[n], x_recv.at[n], side
        )

    def plain(n, up):
        k = 0 if up else 1
        block = wbuf.at[n // 2, n % 2, pl.ds(j * 128, 128)]
        return remote(
            block, block, w_send.at[n, k, 0], w_recv.at[n, k, 0], above if up else below
        )

    def crossed(n, up):
        k = 0 if up else 1
        block = wbuf.at[n // 2, n % 2, pl.ds(jx * 128, 128)]
        return remote(block, block, w_send.at[n, k, 1], w_recv.at[n, k, 0], above if up else below)

    def passed(n, s, up):
        k = 0 if up else 1
        block = wbuf.at[n // 2, n % 2, pl.ds((z - s if up else z + s) * 256, 256)]
        return remote(block, block, w_send.at[n, k, 1 + s], w_recv.at[n, k, s], above if up else below)

    def arrival(n, s, up):
        k = 0 if up else 1
        block = wbuf.at[n // 2, n % 2, pl.ds((z - 1 - s if up else z + 1 + s) * 256, 256)]
        return remote(block, block, w_send.at[n, k, 1 + s], w_recv.at[n, k, s], below if up else above)

    def send_plain(n):
        pl.when(has_up)(lambda: plain(n, True).start())
        pl.when(has_down)(lambda: plain(n, False).start())

    def send_crossed(n):
        block = wbuf.at[n // 2, n % 2, pl.ds(jx * 128, 128)]
        remote(block, block, x_send.at[n], x_recv.at[n], side).wait_recv()
        pl.when(has_up)(lambda: crossed(n, True).start())
        pl.when(has_down)(lambda: crossed(n, False).start())

    def forward(n, s):
        @pl.when(z - 1 - s >= 0)
        def _():
            arrival(n, s, True).wait_recv()
            if s < 2:
                pl.when(has_up)(lambda: passed(n, s + 1, True).start())

        @pl.when(z + 1 + s <= 3)
        def _():
            arrival(n, s, False).wait_recv()
            if s < 2:
                pl.when(has_down)(lambda: passed(n, s + 1, False).start())

    def pump(tick):
        for s in (1, 0):
            if 0 <= tick - s < UNITS:
                forward(tick - s, s)
        n = tick + AHEAD
        if n < UNITS:
            send_plain(n)
            send_crossed(n)
        if n + 2 < UNITS:
            cross(n + 2).start()
        if 0 <= tick - 2 < UNITS:
            forward(tick - 2, 2)

    l_send_out(1)
    tell_second()
    share(z)
    own_w.wait()
    for h in range(2):
        wide[h] = wraw[:, :, halves[h]].reshape(2048, 128).astype(f32)
    regroup(0)
    cross(0).start()
    cross(1).start()
    send_plain(0)
    hear_second()
    l_send_out(2)
    for i in range(1, 4):
        regroup(i)
    hear_third()
    l_send_out(3)
    for n in range(2, AHEAD + 2):
        cross(n).start()
    own_res.wait()
    res_out = remote(resbuf.at[c], resbuf.at[c], half_send.at[2], half_recv.at[2], partner)
    res_in = remote(resbuf.at[c], resbuf.at[1 - c], half_send.at[2], half_recv.at[2], partner)
    res_out.start()

    for copy in small:
        copy.wait()
    for d in range(8):
        pack[d % 2, d // 2] = jnp.concatenate(
            [
                tailc[d].astype(f32),
                inpc[d].astype(f32),
                jnp.full((6, 256), slots[d].astype(f32)),
            ],
            axis=0,
        ).astype(bf16)

    swap_out = remote(pack.at[1 - x], pair.at[:, x], c_send.at[0], c_recv.at[0], side)
    swap_in = remote(pack.at[1 - x], pair.at[:, 1 - x], c_send.at[0], c_recv.at[0], side)
    swap_out.start()
    pair[:, x] = pack[x]

    send_crossed(0)
    send_plain(1)
    send_crossed(1)
    l_step(0)
    relay(z)
    for n in range(2, AHEAD):
        send_plain(n)
        send_crossed(n)
    pump(0)
    l_step(1)
    relay_step(0)
    pump(1)
    l_step(2)
    relay_step(1)
    pump(2)
    relay_step(2)

    def half_copy(gg, index):
        return remote(
            exc.at[gg, c], exc.at[gg, c], half_send.at[index], half_recv.at[index], partner
        )

    def half_arrival(gg, index):
        return remote(
            exc.at[gg, 1 - c], exc.at[gg, 1 - c], half_send.at[index], half_recv.at[index], partner
        )

    for o in range(4):
        share_here(o).wait()
    half_copy(g, 0).start()

    def cache_copy(d):
        peer = lax.rem(z + d, 4)
        return remote(pair.at[peer], cach.at[z], c_send.at[d], c_recv.at[d], at(g, peer * 2 + x, c))

    def cache_arrival(d):
        peer = lax.rem(z + 4 - d, 4)
        return remote(pair.at[0], cach.at[peer], c_send.at[d], c_recv.at[d], at(g, peer * 2 + x, c))

    swap_in.wait_recv()
    for d in range(1, 4):
        cache_copy(d).start()
    cach[z] = pair[z]

    for o in range(4):
        for k, xx in ((0, x), (4, 1 - x)):
            block = exc.at[1 - g, c, :, o, xx]
            remote(block, block, sy_send.at[k + o], sy_recv.at[k + o], across).wait_recv()
    half_copy(1 - g, 1).start()
    pump(3)
    half_arrival(g, 0).wait_recv()
    half_arrival(1 - g, 1).wait_recv()

    routes = {1: (g, 1 - x, side), 2: (1 - g, x, across), 3: (1 - g, 1 - x, corner)}

    def out_block(i, lanes, quarter):
        if i < 2:
            return spin.at[4 * i + quarter]
        return tin.at[4 * i - 8 + quarter, :, lanes]

    def out_copy(r, k):
        i, lanes = parts[k]
        gg, xx, dev = routes[r]
        src = outbox.at[r - 1, i] if i < 2 else outbox.at[r - 1, i, :, lanes]
        return remote(src, out_block(i, lanes, mine), out_send.at[r, k], out_recv.at[r, k], dev)

    def out_arrival(r, k):
        i, lanes = parts[k]
        gg, xx, dev = routes[r]
        block = out_block(i, lanes, 2 * gg + xx)
        return remote(block, block, out_send.at[r, k], out_recv.at[r, k], dev)

    whole = slice(0, 256)
    parts = [(0, whole), (1, whole), (2, halves[0]), (2, halves[1]), (3, halves[0]), (3, halves[1])]

    def spread_of(gg, xx, k):
        i, lanes = parts[k]
        if lanes == whole:
            low = jnp.concatenate([wbuf[i, 0, :512], wbuf[i, 1, :512]], axis=1)
            high = jnp.concatenate([wbuf[i, 0, 512:], wbuf[i, 1, 512:]], axis=1)
        else:
            h = lanes.start // 128
            low, high = wbuf[i, h, :512], wbuf[i, h, 512:]
        value = jnp.dot(exc[gg, 0, xx].reshape(256, 512), low, preferred_element_type=f32)
        value += jnp.dot(exc[gg, 1, xx].reshape(256, 512), high, preferred_element_type=f32)
        return value.astype(bf16)

    def produce(k):
        i, lanes = parts[k]
        for r in (3, 1, 2):
            gg, xx, dev = routes[r]
            outbox[r - 1, i, :, lanes] = spread_of(gg, xx, k)
            out_copy(r, k).start()
        value = spread_of(g, x, k)
        if i < 2:
            spin[4 * i + mine] = value
        else:
            tin[4 * i - 8 + mine, :, lanes] = value

    def placed(row):
        lanes = lax.broadcasted_iota(jnp.int32, (256, 128), 1)
        chosen = jnp.where(lax.rem(lanes, 16) == row, match[...], 0.0).astype(bf16)
        return jnp.dot(chosen, cach[...].reshape(128, 256), preferred_element_type=f32)

    def win_rows(i):
        return pl.ds(0, 6) if i == 0 else pl.ds(6, 4)

    def win_copy(i):
        block = win.at[c, win_rows(i)]
        return remote(block, block, win_send.at[i], win_recv.at[i], partner)

    def win_arrival(i):
        block = win.at[1 - c, win_rows(i)]
        return remote(block, block, win_send.at[i], win_recv.at[i], partner)

    def upsample(i):
        for r in (1, 2, 3):
            out_arrival(r, i).wait_recv()

        @pl.loop(4 * i, 4 * i + 4)
        def _(t):
            value = spin[t].astype(f32) + placed(t) + convb[...]
            ups[t] = value
            win[c, t + 2] = elu32(value).astype(bf16)

        win_copy(i).start()

    def decode(i):
        win_arrival(i).wait_recv()

        @pl.loop(0, 2)
        def _(p):
            t = 4 * i + 2 * p
            branch = jnp.zeros((512, 256), f32) + resb[...]
            for k in range(3):
                for h in range(2):
                    branch = branch + jnp.dot(
                        win[h, pl.ds(t + k, 2)].reshape(512, 256), resbuf[h, k],
                        preferred_element_type=f32,
                    )
            hidden = elu32(branch).astype(bf16)
            value = ups[pl.ds(t, 2)].reshape(512, 256) + jnp.dot(
                hidden, skipw[...], preferred_element_type=f32
            ) + skipb[...]
            for h in range(2):
                rows_dec[h, pl.ds(t, 256, stride=8), :] = value[:256, halves[h]]
                rows_dec[h, pl.ds(t + 1, 256, stride=8), :] = value[256:, halves[h]]

    produce(0)
    pump(4)
    res_in.wait_recv()
    for d in range(1, 4):
        cache_arrival(d).wait_recv()
    named = jnp.broadcast_to(cach[...].reshape(8, 16, 256).astype(f32)[:, 10:11, :], (8, 16, 256)).reshape(128, 256)
    sessions = lax.broadcasted_iota(jnp.int32, (128, 256), 1).astype(f32)
    match[...] = jnp.where(named == sessions, 1.0, 0.0).T
    for i in range(2):
        win[c, i] = placed(8 + i).astype(bf16)
    pump(5)
    produce(1)
    pump(6)
    produce(2)
    pump(7)
    produce(3)
    pump(8)
    produce(4)
    upsample(0)
    pump(9)
    produce(5)
    upsample(1)
    decode(0)
    decode(1)
    for h in range(2):
        dec_ref[:, :, halves[h]] = rows_dec[h].reshape(256, 8, 128).astype(bf16)

    def collect(k):
        i, lanes = parts[k]
        h = lanes.start // 128
        for r in (1, 2, 3):
            out_arrival(r, k).wait_recv()
        for t in range(4 * i - 8, 4 * i - 4):
            rows_tail[h, pl.ds(t, 256, stride=8), :] = tin[t, :, lanes].astype(f32)
        if i == 3:
            tail_ref[:, :, lanes] = rows_tail[h].reshape(256, 8, 128).astype(bf16)

    for k in range(2, 6):
        collect(k)

    for k in range(6):
        for r in (1, 2, 3):
            out_copy(r, k).wait_send()
    for i in range(2):
        win_copy(i).wait_send()
        half_copy((g, 1 - g)[i], i).wait_send()
    res_out.wait_send()
    swap_out.wait_send()
    for d in range(1, 4):
        cache_copy(d).wait_send()
    for o in range(4):
        share_side(o).wait_send()
        share_across(o).wait_send()
        relay_copy(o).wait_send()
    for hops in (1, 2, 3):
        pl.when(z + hops <= 3)(lambda: l_copy(hops, True).wait_send())
        pl.when(z - hops >= 0)(lambda: l_copy(hops, False).wait_send())

    for n in range(UNITS):
        cross(n).wait_send()
        for up, has in ((True, has_up), (False, has_down)):

            @pl.when(has)
            def _():
                plain(n, up).wait_send()
                crossed(n, up).wait_send()
                for s in (1, 2):
                    pl.when((z - s >= 0) if up else (z + s <= 3))(
                        lambda s=s: passed(n, s, up).wait_send()
                    )


def publish(dec_ref, tail_ref, dec_out, tail_out, sem):
    copies = (
        pltpu.make_async_copy(dec_ref, dec_out, sem.at[0]),
        pltpu.make_async_copy(tail_ref, tail_out, sem.at[1]),
    )
    for copy in copies:
        copy.start()
    for copy in copies:
        copy.wait()


def fused(
    latent, conv_weight, conv_bias, tail_cache, input_cache, resume_slot,
    res_weight, res_bias, skip_weight, skip_bias,
):
    dma = pltpu.SemaphoreType.DMA
    bf16, f32 = jnp.bfloat16, jnp.float32
    vmem = pl.BlockSpec(memory_space=pltpu.VMEM)
    anywhere = pl.BlockSpec(memory_space=pl.ANY)
    operands = [
        pltpu.with_memory_space_constraint(array, pltpu.HBM)
        for array in (
            latent, conv_weight, tail_cache, input_cache, resume_slot, conv_bias[None, :], res_weight,
            res_bias[None, :], skip_weight, skip_bias[None, :],
        )
    ]
    decoded, new_tail = pl.pallas_call(
        fused_kernel,
        out_shape=(
            jax.ShapeDtypeStruct((256, 8, 256), bf16),
            jax.ShapeDtypeStruct((256, 8, 256), bf16),
        ),
        in_specs=[anywhere] * 10,
        out_specs=(vmem,) * 2,
        scratch_shapes=[
            pltpu.VMEM((256, 512), bf16),
            pltpu.VMEM((128, 16, 256), bf16),
            pltpu.VMEM((2, 2048, 128), f32),
            pltpu.VMEM((8, 128, 128), bf16),
            pltpu.VMEM((8, 8, 256), bf16),
            pltpu.VMEM((8, 2, 256), bf16),
            pltpu.VMEM((256, 256), bf16),
            pltpu.VMEM((4, 2, 1024, 128), bf16),
            pltpu.VMEM((4, 4, 2, 32, 512), bf16),
            pltpu.VMEM((2, 2, 2, 4, 2, 32, 512), bf16),
            pltpu.VMEM((2, 4, 16, 256), bf16),
            pltpu.VMEM((4, 2, 16, 256), bf16),
            pltpu.VMEM((4, 2, 16, 256), bf16),
            pltpu.VMEM((8, 256, 256), bf16),
            pltpu.VMEM((8, 256, 256), bf16),
            pltpu.VMEM((3, 4, 256, 256), bf16),
            pltpu.VMEM((8, 256, 256), f32),
            pltpu.VMEM((2, 10, 256, 256), bf16),
            pltpu.VMEM((2, 3, 256, 256), bf16),
            pltpu.VMEM((256, 128), f32),
            pltpu.VMEM((2, 2048, 128), f32),
            pltpu.VMEM((2, 2048, 128), f32),
            pltpu.SMEM((8,), jnp.int32),
            pltpu.VMEM((1, 256), f32),
            pltpu.VMEM((1, 256), f32),
            pltpu.VMEM((1, 256), f32),
            dma((8, 2, 4)), dma((8, 2, 3)),
            dma((8,)), dma((8,)),
            dma((4,)), dma((4,)),
            dma((4,)), dma((4,)),
            dma((8,)), dma((8,)),
            dma((3,)), dma((3,)),
            dma((8,)), dma((8,)),
            dma((2,)), dma((2,)),
            dma((4, 6)), dma((4, 6)),
            dma((4,)), dma((10,)), pltpu.SemaphoreType.REGULAR((4,)),
        ],
        compiler_params=pltpu.CompilerParams(
            collective_id=0, has_side_effects=True, vmem_limit_bytes=48 * 1024 * 1024
        ),
    )(*operands)
    return pl.pallas_call(
        publish,
        out_shape=(
            jax.ShapeDtypeStruct((256, 8, 256), bf16),
            jax.ShapeDtypeStruct((256, 8, 256), bf16),
        ),
        in_specs=[vmem] * 2,
        out_specs=(anywhere,) * 2,
        scratch_shapes=[dma((2,))],
    )(*[pltpu.with_memory_space_constraint(array, pltpu.VMEM) for array in (decoded, new_tail)])


def solution(mesh):
    sizes = tuple(mesh.shape[name] for name in ("groups", "streams", "segment"))
    body = fused if sizes == (2, 8, 2) else local
    placed = (
        P(("groups", "streams"), "segment"),
        P("streams", None, "segment"),
        P("segment"),
        P(("groups", "streams"), None, "segment"),
        P(("groups", "streams"), None, "segment"),
        P(("groups", "streams")),
        P(None, "segment", None),
        P(),
        P(None, "segment"),
        P("segment"),
    )
    return jax.shard_map(
        body,
        mesh=mesh,
        in_specs=placed,
        out_specs=(
            P(("groups", "streams"), None, "segment"),
            P(("groups", "streams"), None, "segment"),
        ),
        check_vma=False,
    )
```
